512 devices in a mesh: tok: 32 (over y, x), exp: 16 (over z, core).
Axes of the slice: x: 4, y: 8, z: 8, core: 2. Of those that a mesh axis runs over, the one named last changes fastest.
Arguments:
- tokens: bfloat16 [512, 6144], P('tok', 'exp'), may hold values from -6 to 6
- route_ids: int32 [512, 2], P('tok'), may hold values from 0 to 3, all different within a row; in each aligned block of 16 rows (0 to 15, 16 to 31, ...) at most 12 rows name the same one
- gate_codes: int32 [512, 2], P('tok'), may hold values from 1 to 255
- merge_labels: int32 [4], replicated, may hold values from 0 to 1, as said below
- freq_counts: int32 [4], replicated, may hold values from 1024 to 4096
- w_gate: bfloat16 [32768, 6144], P(('tok', 'exp')), may hold values from -0.078125 to 0.078125
- w_up: bfloat16 [32768, 6144], P(('tok', 'exp')), may hold values from -0.078125 to 0.078125
- w_down: bfloat16 [32768, 6144], P('tok', 'exp'), may hold values from -0.0625 to 0.0625
Outputs:
- initial_out: bfloat16 [512, 6144], P('tok', 'exp')
- merged_out: bfloat16 [512, 6144], P('tok', 'exp')
The draws below stay inside these ranges and needn't reach their ends.
Inputs may be any that keep to these rules, and one draw needn't show every extreme that they name: `route_ids`: the 2 ids of a row differ. Among the 16 rows of one token shard no expert is named more than 12 times, a bound that some block reaches. `merge_labels`: experts with equal labels form one merge group; every group has exactly two experts.
All inputs are finite; a program needn't handle non-finite values.
Results may differ from the reference program's by a relative error of at most 0.0085.
Values may be sent and summed in bfloat16 or wider, within the bound.
A program may use at most 64 MiB of HBM per device.

```python
import math
import jax
import jax.numpy as jnp
import numpy as np

D = 6144
FF = 8192
EXPERTS = 4
TOP = 2
TOK_DEV = 16
CAP = 12
TOKENS = 512
N_TOK = 32


def draw_merge_labels(key, part):
    order = jax.random.permutation(key, EXPERTS)
    position = jnp.argsort(order, stable=True)
    return (position // 2).astype(jnp.int32)


def touch_ends(drawn, own_key, low, top_value):
    place = [jax.random.randint(jax.random.fold_in(own_key, axis), (), 0, length) for axis, length in enumerate(drawn.shape)]
    longest = drawn.shape.index(max(drawn.shape))
    next_to = place[:longest] + [(place[longest] + 1) % drawn.shape[longest]] + place[longest + 1:]
    return drawn.at[tuple(place)].set(low).at[tuple(next_to)].set(top_value)


def shard_levels(rng, shape, pieces, smallest, high):
    def one(dim, blocks):
        draws = jax.random.uniform(jax.random.fold_in(jax.random.fold_in(rng, 6), dim), (blocks,), jnp.float32, smallest / len(pieces), high / len(pieces))
        return jnp.repeat(jnp.exp(draws), shape[dim] // blocks).reshape((-1,) + (1,) * (len(shape) - dim - 1))

    gain = one(*pieces[0])
    for cut in pieces[1:]:
        gain = gain * one(*cut)
    return gain


def deal_out(rng, own, number, rows, number_of, top, most, slope):
    sequence = jax.random.permutation(rng, number_of)
    crowded, ordinary = shares(number_of, rows * top, most, slope, True), shares(number_of, rows * top, most, slope, False)
    places = jnp.arange(number_of)

    def named(sizes, offset_by):
        used = int((sizes > 0).sum())
        fixed = max(1, used // 4)
        moved = fixed + (places - fixed + offset_by * (used - fixed)) % max(1, number_of - fixed)
        return jnp.zeros((number_of,), jnp.int32).at[sequence[jnp.where(places < fixed, places, moved)]].set(jnp.asarray(sizes, jnp.int32))

    sizes = jnp.where(number % 4 == 0, named(crowded, number // 4), named(ordinary, number - number // 4 - 1))
    mixed = jax.random.permutation(jax.random.fold_in(own, 3), number_of)
    giver, taker = mixed[0:number_of // 2 * 2:2], mixed[1:number_of // 2 * 2:2]
    margin = jnp.minimum(sizes[giver] - 1, most - sizes[taker]) // 2
    margin = jnp.where((giver == sequence[0]) | (taker == sequence[0]) | (sizes[taker] == 0), 0, jnp.maximum(margin, 0))
    moved = jax.random.randint(jax.random.fold_in(own, 4), (number_of // 2,), 0, 1 << 20) % (margin + 1)
    sizes = sizes.at[giver].add(-moved).at[taker].add(moved)
    items = jnp.searchsorted(jnp.cumsum(sizes), jnp.arange(rows * top), side="right").astype(jnp.int32)
    listing = items.reshape(top, rows).T
    listing = listing[jax.random.permutation(jax.random.fold_in(own, 1), rows)]
    offset_by = jax.random.randint(jax.random.fold_in(own, 2), (rows, 1), 0, top)
    return jnp.take_along_axis(listing, (jnp.arange(top)[None, :] + offset_by) % top, axis=1)


def shares(count, total, limit, skew, full):
    loads = [(1 << 20) // math.isqrt(grade ** skew) + 1 for grade in range(1, count + 1)]
    largest = limit if full else min(limit, max(-(-total // count), total * loads[0] // sum(loads)))
    least = 1 if total - largest >= count - 1 else 0
    counts, spare = [largest] + [least] * (count - 1), total - largest - least * (count - 1)
    while spare > 0:
        movable = [i for i in range(1, count) if counts[i] < largest] or [i for i in range(1, count) if counts[i] < limit]
        pool, budget = sum([loads[i] for i in movable]), spare
        for i in movable:
            addition = min(limit - counts[i], max(1, budget * loads[i] // pool), spare)
            counts[i] = counts[i] + addition
            spare = spare - addition
    return np.array(counts)


def scatter_about(rng, dims, width, bound, cuts=(), held_as=jnp.bfloat16):
    entries = jax.random.normal(rng, dims, jnp.float32) * width
    if len(cuts) > 0:
        entries = shard_levels(rng, dims, cuts, -0.22, 0.18) * entries
    return jnp.clip(entries, min=-bound, max=bound).astype(held_as)


def setup_inputs(seed: int = 0) -> dict:
    key_list = jax.random.split(jax.random.key(seed), 9)
    tokens = scatter_about(key_list[0], (TOKENS, D), 1.0, 6.0, ((0, 32), (1, 16)))
    route_ids_keys = jax.random.split(jax.random.fold_in(key_list[1], 1), TOKENS // TOK_DEV)
    route_ids_turns = jax.random.permutation(jax.random.fold_in(key_list[1], 3), TOKENS // TOK_DEV)
    route_ids = jax.vmap(lambda own, number: deal_out(jax.random.fold_in(key_list[1], 2), own, number, TOK_DEV, EXPERTS, TOP, CAP, 2))(route_ids_keys, route_ids_turns).reshape((TOKENS, TOP))
    gate_codes = touch_ends(jax.random.randint(key_list[2], (TOKENS, TOP), 1, 256), jax.random.fold_in(key_list[2], 1), 1, 255).astype(jnp.int32)
    merge_labels = draw_merge_labels(jax.random.fold_in(key_list[8], 71), 0)
    freq_counts = touch_ends(jax.random.randint(key_list[4], (EXPERTS,), 1024, 4097), jax.random.fold_in(key_list[4], 1), 1024, 4096).astype(jnp.int32)
    w_gate = scatter_about(key_list[5], (EXPERTS * FF, D), D ** -0.5, 0.078125, ((0, 512),))
    w_up = scatter_about(key_list[6], (EXPERTS * FF, D), D ** -0.5, 0.078125, ((0, 512),))
    w_down = scatter_about(key_list[7], (EXPERTS * FF, D), FF ** -0.5, 0.0625, ((0, 32), (1, 16)))
    return {"tokens": tokens, "route_ids": route_ids, "gate_codes": gate_codes, "merge_labels": merge_labels, "freq_counts": freq_counts, "w_gate": w_gate, "w_up": w_up, "w_down": w_down}


def slots_of(route_ids):
    flat = route_ids.reshape(N_TOK, TOK_DEV * TOP)
    picked = (flat[..., None] == jnp.arange(EXPERTS, dtype=jnp.int32)).astype(jnp.int32)
    before = jnp.cumsum(picked, axis=1) - picked
    return jnp.sum(before * picked, axis=2).reshape(N_TOK * TOK_DEV, TOP).astype(jnp.int32)


def swiglu(rows, gate_w, up_w, down_w):
    gate = jnp.dot(rows, gate_w.T, preferred_element_type=jnp.float32)
    upper = jnp.dot(rows, up_w.T, preferred_element_type=jnp.float32)
    hidden = (jax.nn.silu(gate) * upper).astype(jnp.bfloat16)
    return jnp.dot(hidden, down_w, preferred_element_type=jnp.float32)


def reference(tokens, route_ids, gate_codes, merge_labels, freq_counts, w_gate, w_up, w_down):
    slot = slots_of(route_ids)
    shard = (jnp.arange(N_TOK * TOK_DEV, dtype=jnp.int32) // TOK_DEV)[:, None]
    position = (shard * CAP + slot).astype(jnp.int32)
    scale = gate_codes.astype(jnp.float32) / 256.0
    freq = freq_counts.astype(jnp.float32)
    total_rows = N_TOK * CAP
    orig_acc = jnp.zeros((N_TOK * TOK_DEV, D), jnp.float32)
    merged_acc = jnp.zeros((N_TOK * TOK_DEV, D), jnp.float32)
    for expert in range(EXPERTS):
        chosen = route_ids == expert
        target = jnp.where(chosen, position, total_rows).astype(jnp.int32)
        rows = jnp.zeros((total_rows + 1, D), jnp.bfloat16)
        rows = rows.at[target.reshape(-1)].set(jnp.repeat(tokens, TOP, axis=0))[:total_rows]
        member = jnp.where(merge_labels == merge_labels[expert], freq, jnp.float32(0.0))
        coef = member / jnp.sum(member)
        merged = []
        for which in range(3):
            accum = jnp.zeros((FF, D), jnp.float32)
            for other in range(EXPERTS):
                if which == 0:
                    block = w_gate[other * FF:(other + 1) * FF, :]
                elif which == 1:
                    block = w_up[other * FF:(other + 1) * FF, :]
                else:
                    block = w_down[other * FF:(other + 1) * FF, :]
                accum = accum + coef[other] * block.astype(jnp.float32)
            merged.append(accum.astype(jnp.bfloat16))
        y_orig = swiglu(rows, w_gate[expert * FF:(expert + 1) * FF, :], w_up[expert * FF:(expert + 1) * FF, :], w_down[expert * FF:(expert + 1) * FF, :])
        y_merged = swiglu(rows, merged[0], merged[1], merged[2])
        safe = jnp.minimum(target, total_rows - 1)
        weight = jnp.where(chosen, scale, jnp.float32(0.0))[:, :, None]
        orig_acc = orig_acc + jnp.sum(weight * y_orig[safe], axis=1)
        merged_acc = merged_acc + jnp.sum(weight * y_merged[safe], axis=1)
    return orig_acc.astype(jnp.bfloat16), merged_acc.astype(jnp.bfloat16)
```

```python
import jax
import jax.numpy as jnp
from jax import lax
from jax.sharding import PartitionSpec as P

EXPERTS = 4
LANES = 128


def local(tokens, route_ids, gate_codes, merge_labels, freq_counts, w_gate, w_up, w_down):
    n_tok = lax.axis_size("tok")
    span = n_tok // EXPERTS
    expert = lax.axis_index("tok") // span
    tok_dev, width = tokens.shape
    units = w_gate.shape[0]
    ids = jnp.arange(LANES, dtype=jnp.int32)
    scale = gate_codes.astype(jnp.float32) / 256.0
    share = jnp.sum(jnp.where(route_ids[:, :, None] == ids, scale[:, :, None], 0.0), axis=1)
    wide = lax.all_gather(tokens, "exp", axis=1, tiled=True)
    wide = jnp.concatenate([wide, share.astype(jnp.bfloat16)], axis=1)
    every = lax.all_gather(wide, "tok", axis=0, tiled=True)
    depth = every.shape[1] - LANES
    rows, share = every[:, :depth], every[:, depth : depth + EXPERTS].astype(jnp.float32)

    freq = freq_counts.astype(jnp.float32)
    experts = jnp.arange(EXPERTS, dtype=jnp.int32)
    own_label = jnp.sum(jnp.where(experts == expert, merge_labels, 0))
    member = merge_labels == own_label
    total = jnp.sum(jnp.where(member, freq, 0.0))
    own = jnp.sum(jnp.where(experts == expert, freq, 0.0)) / total
    other = jnp.sum(jnp.where(member & (experts != expert), freq, 0.0)) / total

    both = jnp.concatenate([w_gate, w_up], axis=0)
    first = jnp.einsum("nd,fd->nf", rows, both, preferred_element_type=jnp.float32)
    partner = jnp.where(
        merge_labels[1] == merge_labels[0], 0, jnp.where(merge_labels[2] == merge_labels[0], 1, 2)
    )

    def swap(mask):
        def run(value):
            pairs = [(i, (((i // span) ^ mask) * span) + i % span) for i in range(n_tok)]
            return lax.ppermute(value, "tok", pairs)

        return run

    sent = first.astype(jnp.bfloat16)
    got = lax.switch(partner, [swap(1), swap(2), swap(3)], sent)
    merged = own * first + other * got.astype(jnp.float32)

    def act(v):
        return (jax.nn.silu(v[:, :units]) * v[:, units:]).astype(jnp.bfloat16)

    hidden = jnp.concatenate([act(first), act(merged)], axis=0)
    hidden = lax.all_gather(hidden, "exp", axis=1, tiled=True)
    out = jnp.dot(hidden, w_down, preferred_element_type=jnp.float32)
    take_own = jnp.sum(jnp.where(experts == expert, share, 0.0), axis=1)
    take_group = own * jnp.sum(jnp.where(member, share, 0.0), axis=1)
    weight = jnp.concatenate([take_own, take_group])
    out = (out * weight[:, None]).astype(jnp.bfloat16)
    out = out.reshape(2, n_tok, tok_dev, width)
    out = lax.all_to_all(out, "tok", split_axis=1, concat_axis=1, tiled=True)
    out = jnp.sum(out.astype(jnp.float32), axis=1).astype(jnp.bfloat16)
    return out[0], out[1]


def solution(mesh):
    return jax.shard_map(
        local,
        mesh=mesh,
        in_specs=(
            P("tok", "exp"),
            P("tok", None),
            P("tok", None),
            P(),
            P(),
            P(("tok", "exp"), None),
            P(("tok", "exp"), None),
            P("tok", "exp"),
        ),
        out_specs=(P("tok", "exp"), P("tok", "exp")),
        check_vma=False,
    )
```

```python
import functools

import jax
import jax.numpy as jnp
from jax import lax
from jax.experimental import pallas as pl
from jax.experimental.pallas import tpu as pltpu
from jax.sharding import PartitionSpec as P

EXPERTS = 4
LANES = 128
NX, NY, NZ = 4, 8, 8
MESH = pl.DeviceIdType.MESH
BF16, F32 = jnp.bfloat16, jnp.float32
ORDER = (0, -1, 1, -2, 2, -3, 3, -4)
UP_STEPS, DOWN_STEPS = 4, 3


def kernel(
    flip, labels, freq, tokens, share, w_gate, w_up, w_down, first_out, second_out,
    rows, wcat, wd, part, part_in, full, swap, swap_in, hid, ysend, yrecv, yown, xsend, xrecv, fsend, frecv,
    t_loc, w_loc, w_snd, w_rcv, z_snd, z_rcv, up_snd, up_rcv, dn_snd, dn_rcv,
    xr_snd, xr_rcv, xl_snd, xl_rcv, fr_snd, fr_rcv, fl_snd, fl_rcv,
    p_snd, p_rcv, e_snd, e_rcv, h_snd, h_rcv, y_snd, y_rcv, x_snd, x_rcv, f_snd, f_rcv,
):
    tok, exp = lax.axis_index("tok"), lax.axis_index("exp")
    y, x = tok // NX, tok % NX
    z, core = exp // 2, exp % 2
    sib = (tok, z * 2 + (1 - core))
    half = w_gate.shape[0]
    units = 2 * half
    tok_dev, width = tokens.shape
    planes = width // LANES
    total = NZ * planes + 1
    span = NX * tok_dev
    expert = y // 2

    def at_z(k):
        return (tok, ((z + k) % NZ) * 2 + core)

    def at_y(k):
        return (((y + k) % NY) * NX + x, exp)

    def at_x(k):
        return (y * NX + (x + k) % NX, exp)

    def remote(src, dst, snd, rcv, dev):
        return pltpu.make_async_remote_copy(
            src_ref=src, dst_ref=dst, send_sem=snd, recv_sem=rcv, device_id=dev, device_id_type=MESH
        )

    def rows_of(t, lo=0, n=None):
        n = total if n is None else n
        return rows.at[pl.ds(lo, n), pl.ds(pl.multiple_of(t * tok_dev, tok_dev), tok_dev), :]

    mine = pl.ds(pl.multiple_of(tok * tok_dev, tok_dev), tok_dev)
    locals_ = []
    for i in range(planes):
        locals_.append(
            pltpu.make_async_copy(
                tokens.at[:, pl.ds(i * LANES, LANES)], rows.at[z * planes + i, mine, :], t_loc.at[i]
            )
        )
    locals_.append(pltpu.make_async_copy(share, rows.at[NZ * planes, mine, :], t_loc.at[planes]))
    for copy in locals_:
        copy.start()

    barrier = pltpu.get_barrier_semaphore()
    greeted = [at_z(k) for k in range(1, NZ)] + [at_y(k) for k in range(1, NY)]
    greeted += [at_x(k) for k in range(1, NX)] + [sib]
    for dev in greeted:
        pl.semaphore_signal(barrier, inc=1, device_id=dev, device_id_type=MESH)

    loads = []
    for zz in range(NZ):
        for which, ref in enumerate((w_gate, w_up)):
            dst = wcat.at[zz, pl.ds(pl.multiple_of(which * units + core * half, half), half), :]
            cols = pl.ds(pl.multiple_of((2 * zz + core) * width, LANES), width)
            loads.append(pltpu.make_async_copy(ref.at[:, cols], dst, w_loc.at[2 * zz + which]))
    wide = pl.ds(pl.multiple_of(core * width, LANES), width)
    loads.append(pltpu.make_async_copy(w_down, wd.at[:, wide], w_loc.at[2 * NZ]))
    for copy in loads:
        copy.start()
    for copy in locals_:
        copy.wait()
    pl.semaphore_wait(barrier, len(greeted))

    zs = []
    own_planes = rows.at[pl.ds(z * planes, planes), mine, :]
    for k in (1, 7, 2, 6, 3, 5, 4):
        zs.append(remote(own_planes, own_planes, z_snd.at[k], z_rcv.at[k], at_z(k)))
    for copy in zs:
        copy.start()

    gifts = []
    for zz in range(NZ):
        for which, ref in enumerate((w_gate, w_up)):
            dst = wcat.at[zz, pl.ds(pl.multiple_of(which * units + core * half, half), half), :]
            cols = pl.ds(pl.multiple_of((2 * zz + (1 - core)) * width, LANES), width)
            i = 2 * zz + which
            gifts.append(remote(ref.at[:, cols], dst, w_snd.at[i], w_rcv.at[i], sib))
    gifts.append(remote(w_down, wd.at[:, wide], w_snd.at[2 * NZ], w_rcv.at[2 * NZ], sib))
    for copy in gifts:
        copy.start()

    for k in range(1, NZ):
        got = rows.at[pl.ds(((z - k) % NZ) * planes, planes), mine, :]
        remote(got, got, z_snd.at[k], z_rcv.at[k], at_z(k)).wait_recv()

    def group(k):
        return (y + ORDER[k]) % NY

    sent = []

    def send(*args):
        copy = remote(*args)
        copy.start()
        sent.append(copy)

    def along_y(k):
        block = rows_of(group(k) * NX + x)
        off = ORDER[k]
        if off <= 0 and -off < UP_STEPS:
            send(block, block, up_snd.at[-off], up_rcv.at[-off], at_y(1))
        if off >= 0 and off < DOWN_STEPS:
            send(block, block, dn_snd.at[off], dn_rcv.at[off], at_y(-1))

    def from_y(k):
        block = rows_of(group(k) * NX + x)
        off = ORDER[k]
        if off < 0:
            remote(block, block, up_snd.at[-off - 1], up_rcv.at[-off - 1], at_y(1)).wait_recv()
        elif off > 0:
            remote(block, block, dn_snd.at[off - 1], dn_rcv.at[off - 1], at_y(-1)).wait_recv()

    def along_x(k):
        block = rows_of(group(k) * NX + x)
        send(block, block, xr_snd.at[k], xr_rcv.at[k], at_x(1))
        send(block, block, xl_snd.at[k], xl_rcv.at[k], at_x(-1))

    low = total // 2

    def from_x(k):
        left = rows_of(group(k) * NX + (x - 1) % NX)
        remote(left, left, xr_snd.at[k], xr_rcv.at[k], at_x(1)).wait_recv()
        piece = rows_of(group(k) * NX + (x - 1) % NX, 0, low)
        send(piece, piece, fr_snd.at[k], fr_rcv.at[k], at_x(1))
        right = rows_of(group(k) * NX + (x + 1) % NX)
        remote(right, right, xl_snd.at[k], xl_rcv.at[k], at_x(-1)).wait_recv()
        piece = rows_of(group(k) * NX + (x + 1) % NX, low, total - low)
        send(piece, piece, fl_snd.at[k], fl_rcv.at[k], at_x(-1))

    def from_far(k):
        piece = rows_of(group(k) * NX + (x + 2) % NX, 0, low)
        remote(piece, piece, fr_snd.at[k], fr_rcv.at[k], at_x(1)).wait_recv()
        piece = rows_of(group(k) * NX + (x + 2) % NX, low, total - low)
        remote(piece, piece, fl_snd.at[k], fl_rcv.at[k], at_x(-1)).wait_recv()

    def span_of(k):
        return pl.ds(pl.multiple_of(group(k) * span, span), span)

    nt = (((1,), (1,)), ((), ()))

    def multiply(k):
        here = span_of(k)
        acc = jnp.zeros((span, 2 * units), F32)
        for j in range(NZ * planes // 2):
            a, b = 2 * j, 2 * j + 1
            lhs = jnp.concatenate([rows[a, here, :], rows[b, here, :]], axis=1)
            rhs = jnp.concatenate(
                [
                    wcat[a // planes, :, (a % planes) * LANES : (a % planes + 1) * LANES],
                    wcat[b // planes, :, (b % planes) * LANES : (b % planes + 1) * LANES],
                ],
                axis=1,
            )
            acc = acc + lax.dot_general(lhs, rhs, nt, preferred_element_type=F32)
        part[here, :] = acc
        send(part.at[here, :], part_in.at[here, :], p_snd.at[k], p_rcv.at[k], sib)

    partner_tok = (((expert ^ flip) * 2 + (y % 2)) * NX) + x

    def joined(k):
        here = span_of(k)
        remote(part.at[here, :], part_in.at[here, :], p_snd.at[k], p_rcv.at[k], sib).wait_recv()
        both = part[here, :] + part_in[here, :]
        full[here, :] = both
        swap[here, :] = both.astype(BF16)

    def swap_copy(k):
        here = span_of(k)
        g = group(k)
        return remote(swap.at[here, :], swap_in.at[here, :], e_snd.at[g], e_rcv.at[g], (partner_tok, exp))

    def to_partner(k):
        @pl.when(core == 1)
        def _():
            swap_copy(k).start()

    lane = lax.broadcasted_iota(jnp.int32, (1, LANES), 1)
    zero = jnp.zeros((1, LANES), F32)
    freq_v, label_v = zero, jnp.full((1, LANES), -1, jnp.int32)
    own_label = jnp.int32(0)
    for e in range(EXPERTS):
        freq_v = jnp.where(lane == e, freq[e].astype(F32), freq_v)
        label_v = jnp.where(lane == e, labels[e], label_v)
        own_label = jnp.where(expert == e, labels[e], own_label)
    member = jnp.where(label_v == own_label, 1.0, 0.0).astype(F32)
    member_freq = member * freq_v
    coef = member_freq / jnp.sum(member_freq, axis=1, keepdims=True)
    own_lane = jnp.where(lane == expert, 1.0, 0.0).astype(F32)
    own = jnp.sum(coef * own_lane, axis=1, keepdims=True)
    other = jnp.sum(coef * (1.0 - own_lane), axis=1, keepdims=True)
    taken = jnp.where(core == 1, own * member, own_lane)

    def activate(k):
        here = span_of(k)

        @pl.when(core == 1)
        def _():
            swap_copy(k).wait_recv()
            v = own * full[here, :] + other * swap_in[here, :].astype(F32)
            full[here, :] = v

        v = full[here, :]
        gate, upper = v[:, :units], v[:, units:]
        hid[z, here, :] = (gate / (1.0 + jnp.exp(-gate)) * upper).astype(BF16)

    def along_z(k):
        here = span_of(k)
        for d in (4, 3, 5, 2, 6, 1, 7):
            remote(hid.at[z, here, :], hid.at[z, here, :], h_snd.at[k], h_rcv.at[k], at_z(d)).start()

    def finish(k):
        here = span_of(k)
        seven = hid.at[pl.ds(0, NZ - 1), here, :]
        pltpu.make_async_copy(seven, seven, h_rcv.at[k]).wait()
        acc = jnp.zeros((span, 2 * width), F32)
        for j in range(NZ // 2):
            lhs = jnp.concatenate([hid[2 * j, here, :], hid[2 * j + 1, here, :]], axis=1)
            acc = acc + jnp.dot(
                lhs, wd[2 * j * units : 2 * (j + 1) * units, :], preferred_element_type=F32
            )
        weight = jnp.sum(rows[NZ * planes, here, :].astype(F32) * taken, axis=1, keepdims=True)
        acc = acc * weight
        if k == 0:
            yown[...] = acc
        else:
            ysend[k] = acc.astype(BF16)
            send(ysend.at[k], yrecv.at[k], y_snd.at[k], y_rcv.at[k], at_y(ORDER[k]))

    along_y(0)
    along_x(0)
    for copy in loads:
        copy.wait()
    for k in range(NY):
        if k + 1 < NY:
            from_y(k + 1)
            along_y(k + 1)
            along_x(k + 1)
        from_x(k)
        if k == 1:
            for zz in range(NZ):
                for which in range(2):
                    i = 2 * zz + which
                    dst = wcat.at[zz, pl.ds(pl.multiple_of(which * units + (1 - core) * half, half), half), :]
                    remote(dst, dst, w_snd.at[i], w_rcv.at[i], sib).wait_recv()
        if k >= 1:
            from_far(k - 1)
            multiply(k - 1)
        if k >= 2:
            joined(k - 2)
            if k >= 3:
                to_partner(k - 3)
    from_far(NY - 1)
    multiply(NY - 1)
    joined(NY - 2)
    to_partner(NY - 3)
    joined(NY - 1)
    to_partner(NY - 2)
    theirs = wd.at[:, pl.ds(pl.multiple_of((1 - core) * width, LANES), width)]
    remote(theirs, theirs, w_snd.at[2 * NZ], w_rcv.at[2 * NZ], sib).wait_recv()
    to_partner(NY - 1)
    for k in range(NY):
        activate(k)
        if k >= 1:
            along_z(k - 1)
        if k >= 3:
            finish(k - 3)
    along_z(NY - 1)
    for k in range(NY - 3, NY):
        finish(k)

    acc = yown[...]
    for k in range(1, NY):
        remote(ysend.at[k], yrecv.at[k], y_snd.at[k], y_rcv.at[k], at_y(ORDER[k])).wait_recv()
        acc = acc + yrecv[k].astype(F32)
    xsend[...] = acc.astype(BF16).reshape(NX, tok_dev, 2 * width)
    yown[...] = acc
    for k in range(1, NX):
        send(xsend.at[(x + k) % NX], xrecv.at[k], x_snd.at[k], x_rcv.at[k], at_x(k))
    acc = yown[pl.ds(pl.multiple_of(x * tok_dev, tok_dev), tok_dev), :]
    for k in range(1, NX):
        remote(xsend.at[0], xrecv.at[k], x_snd.at[k], x_rcv.at[k], at_x(k)).wait_recv()
        acc = acc + xrecv[k].astype(F32)
    kept = jnp.where(core == 0, acc[:, :width], acc[:, width:]).astype(BF16)
    fsend[...] = jnp.where(core == 0, acc[:, width:], acc[:, :width]).astype(BF16)
    send(fsend, frecv, f_snd, f_rcv, sib)
    remote(fsend, frecv, f_snd, f_rcv, sib).wait_recv()
    back = frecv[...]
    first_out[...] = jnp.where(core == 0, kept, back)
    second_out[...] = jnp.where(core == 0, back, kept)

    for copy in zs + gifts + sent:
        copy.wait_send()
    for k in range(NY):
        seven = hid.at[pl.ds(0, NZ - 1), span_of(k), :]
        pltpu.make_async_copy(seven, seven, h_snd.at[k]).wait()

    @pl.when(core == 1)
    def _():
        for k in range(NY):
            swap_copy(k).wait_send()


def local(tokens, route_ids, gate_codes, merge_labels, freq_counts, w_gate, w_up, w_down):
    ids = jnp.arange(LANES, dtype=jnp.int32)
    scale = gate_codes.astype(F32) / 256.0
    share = jnp.sum(jnp.where(route_ids[:, :, None] == ids, scale[:, :, None], 0.0), axis=1)
    share = share.astype(BF16)
    tok_dev, width = tokens.shape
    half = w_gate.shape[0]
    count, depth = NX * NY * tok_dev, w_down.shape[0]
    units = 2 * half
    planes = width // LANES
    span = NX * tok_dev
    dma = pltpu.SemaphoreType.DMA
    scratch = [
        pltpu.VMEM((NZ * planes + 1, count, LANES), BF16),
        pltpu.VMEM((NZ, 2 * units, width), BF16),
        pltpu.VMEM((depth, 2 * width), BF16),
        pltpu.VMEM((count, 2 * units), F32),
        pltpu.VMEM((count, 2 * units), F32),
        pltpu.VMEM((count, 2 * units), F32),
        pltpu.VMEM((count, 2 * units), BF16),
        pltpu.VMEM((count, 2 * units), BF16),
        pltpu.VMEM((NZ, count, units), BF16),
        pltpu.VMEM((NY, span, 2 * width), BF16),
        pltpu.VMEM((NY, span, 2 * width), BF16),
        pltpu.VMEM((span, 2 * width), F32),
        pltpu.VMEM((NX, tok_dev, 2 * width), BF16),
        pltpu.VMEM((NX, tok_dev, 2 * width), BF16),
        pltpu.VMEM((tok_dev, width), BF16),
        pltpu.VMEM((tok_dev, width), BF16),
        dma((planes + 1,)),
        dma((2 * NZ + 1,)),
        dma((2 * NZ + 1,)),
        dma((2 * NZ + 1,)),
        dma((NZ,)),
        dma((NZ,)),
        *[dma((NY // 2,))] * 4,
        *[dma((NY,))] * 16,
        dma((NX,)),
        dma((NX,)),
        dma(()),
        dma(()),
    ]
    smem, hbm = pl.BlockSpec(memory_space=pltpu.SMEM), pl.BlockSpec(memory_space=pl.ANY)
    vmem = pl.BlockSpec(memory_space=pltpu.VMEM)
    out = jax.ShapeDtypeStruct((tok_dev, width), BF16)

    def variant(flip):
        def run(*args):
            return pl.pallas_call(
                functools.partial(kernel, flip),
                out_shape=(out, out),
                in_specs=[smem, smem, hbm, hbm, hbm, hbm, hbm],
                out_specs=(vmem, vmem),
                scratch_shapes=scratch,
                compiler_params=pltpu.CompilerParams(
                    collective_id=flip, has_side_effects=True, vmem_limit_bytes=40 * 1024 * 1024
                ),
                name=f"layer_flip{flip}",
            )(*args)

        return run

    same = merge_labels[1:] == merge_labels[0]
    pairing = jnp.where(same[0], 0, jnp.where(same[1], 1, 2))
    return lax.switch(
        pairing,
        [variant(1), variant(2), variant(3)],
        merge_labels, freq_counts, tokens, share, w_gate, w_up, w_down,
    )


def solution(mesh):
    return jax.shard_map(
        local,
        mesh=mesh,
        in_specs=(
            P("tok", "exp"),
            P("tok", None),
            P("tok", None),
            P(),
            P(),
            P(("tok", "exp"), None),
            P(("tok", "exp"), None),
            P("tok", "exp"),
        ),
        out_specs=(P("tok", "exp"), P("tok", "exp")),
        check_vma=False,
    )
```

```python
import functools

import jax
import jax.numpy as jnp
from jax import lax
from jax.experimental import pallas as pl
from jax.experimental.pallas import tpu as pltpu
from jax.sharding import PartitionSpec as P

EXPERTS = 4
LANES = 128
NX, NY, NZ = 4, 8, 8
MESH = pl.DeviceIdType.MESH
BF16, F32 = jnp.bfloat16, jnp.float32
ORDER = (0, -1, 1, -2, 2, -3, 3, -4)
UP_STEPS, DOWN_STEPS = 4, 3
PAIR_ORDER = {
    2: ((1, 0, 2, -1, 3, -3, -2, -4), (5, 6, 7, 8, 9, 9, 10, 10)),
    -2: ((-1, -2, 0, -3, 1, 3, -4, 2), (5, 6, 7, 8, 9, 9, 10, 10)),
    4: ((2, -2, 1, -3, -1, 3, 0, -4), (7, 7, 8, 8, 9, 9, 10, 10)),
}
LAG = 2


def kernel(
    flip, labels, freq, ids, codes, tokens, w_gate, w_up, w_down, first_out, second_out,
    rows, wcat, wd, part, part_in, full, swap, swap_in, hid, ysend, yrecv, yown, xsend, xrecv, fsend, frecv,
    t_loc, w_loc, w_snd, w_rcv, z_snd, z_rcv, up_snd, up_rcv, dn_snd, dn_rcv,
    xr_snd, xr_rcv, xl_snd, xl_rcv, fr_snd, fr_rcv, fl_snd, fl_rcv,
    p_snd, p_rcv, e_snd, e_rcv, h_snd, h_rcv, y_snd, y_rcv, x_snd, x_rcv, f_snd, f_rcv,
):
    tok, exp = lax.axis_index("tok"), lax.axis_index("exp")
    y, x = tok // NX, tok % NX
    z, core = exp // 2, exp % 2
    sib = (tok, z * 2 + (1 - core))
    half = w_gate.shape[0]
    units = 2 * half
    tok_dev, width = tokens.shape
    planes = width // LANES
    total = NZ * planes + 1
    span = NX * tok_dev
    expert = y // 2

    def at_z(k):
        return (tok, ((z + k) % NZ) * 2 + core)

    def at_y(k):
        return (((y + k) % NY) * NX + x, exp)

    def at_x(k):
        return (y * NX + (x + k) % NX, exp)

    def remote(src, dst, snd, rcv, dev):
        return pltpu.make_async_remote_copy(
            src_ref=src, dst_ref=dst, send_sem=snd, recv_sem=rcv, device_id=dev, device_id_type=MESH
        )

    def rows_of(t, lo=0, n=None):
        n = total if n is None else n
        return rows.at[pl.ds(lo, n), pl.ds(pl.multiple_of(t * tok_dev, tok_dev), tok_dev), :]

    mine = pl.ds(pl.multiple_of(tok * tok_dev, tok_dev), tok_dev)
    locals_ = []
    for i in range(planes):
        locals_.append(
            pltpu.make_async_copy(
                tokens.at[:, pl.ds(i * LANES, LANES)], rows.at[z * planes + i, mine, :], t_loc.at[i]
            )
        )
    for copy in locals_:
        copy.start()

    lane = lax.broadcasted_iota(jnp.int32, (tok_dev, LANES), 1)
    diag = lax.broadcasted_iota(jnp.int32, (tok_dev, tok_dev), 0) == lax.broadcasted_iota(
        jnp.int32, (tok_dev, tok_dev), 1
    )
    share = jnp.zeros((tok_dev, LANES), F32)
    for e in range(EXPERTS):
        line = jnp.sum(jnp.where(ids[...] == e, codes[...].astype(F32) / 256.0, 0.0), axis=0, keepdims=True)
        column = jnp.sum(jnp.where(diag, jnp.broadcast_to(line, diag.shape), 0.0), axis=1, keepdims=True)
        share = share + jnp.where(lane == e, column, 0.0)
    rows[NZ * planes, mine, :] = share.astype(BF16)

    barrier = pltpu.get_barrier_semaphore()
    greeted = [at_z(k) for k in range(1, NZ)] + [at_y(k) for k in range(1, NY)]
    greeted += [at_x(k) for k in range(1, NX)] + [sib]
    for dev in greeted:
        pl.semaphore_signal(barrier, inc=1, device_id=dev, device_id_type=MESH)

    loads = []
    for zz in range(NZ):
        for which, ref in enumerate((w_gate, w_up)):
            dst = wcat.at[zz, pl.ds(pl.multiple_of(which * units + core * half, half), half), :]
            cols = pl.ds(pl.multiple_of((2 * zz + core) * width, LANES), width)
            loads.append(pltpu.make_async_copy(ref.at[:, cols], dst, w_loc.at[2 * zz + which]))
    wide = pl.ds(pl.multiple_of(core * width, LANES), width)
    loads.append(pltpu.make_async_copy(w_down, wd.at[:, wide], w_loc.at[2 * NZ]))
    for copy in loads:
        copy.start()
    for copy in locals_:
        copy.wait()
    pl.semaphore_wait(barrier, len(greeted))

    zs = []
    own_planes = rows.at[pl.ds(z * planes, planes), mine, :]
    for k in (1, 7, 2, 6, 3, 5, 4):
        zs.append(remote(own_planes, own_planes, z_snd.at[k], z_rcv.at[k], at_z(k)))
    for copy in zs:
        copy.start()

    gifts = []
    for zz in range(NZ):
        for which, ref in enumerate((w_gate, w_up)):
            dst = wcat.at[zz, pl.ds(pl.multiple_of(which * units + core * half, half), half), :]
            cols = pl.ds(pl.multiple_of((2 * zz + (1 - core)) * width, LANES), width)
            i = 2 * zz + which
            gifts.append(remote(ref.at[:, cols], dst, w_snd.at[i], w_rcv.at[i], sib))
    gifts.append(remote(w_down, wd.at[:, wide], w_snd.at[2 * NZ], w_rcv.at[2 * NZ], sib))
    for copy in gifts:
        copy.start()

    for k in range(1, NZ):
        got = rows.at[pl.ds(((z - k) % NZ) * planes, planes), mine, :]
        remote(got, got, z_snd.at[k], z_rcv.at[k], at_z(k)).wait_recv()

    def group(k):
        return (y + ORDER[k]) % NY

    sent = []

    def send(*args):
        copy = remote(*args)
        copy.start()
        sent.append(copy)

    def along_y(k):
        block = rows_of(group(k) * NX + x)
        off = ORDER[k]
        if off <= 0 and -off < UP_STEPS:
            send(block, block, up_snd.at[-off], up_rcv.at[-off], at_y(1))
        if off >= 0 and off < DOWN_STEPS:
            send(block, block, dn_snd.at[off], dn_rcv.at[off], at_y(-1))

    def from_y(k):
        block = rows_of(group(k) * NX + x)
        off = ORDER[k]
        if off < 0:
            remote(block, block, up_snd.at[-off - 1], up_rcv.at[-off - 1], at_y(1)).wait_recv()
        elif off > 0:
            remote(block, block, dn_snd.at[off - 1], dn_rcv.at[off - 1], at_y(-1)).wait_recv()

    def along_x(k):
        block = rows_of(group(k) * NX + x)
        send(block, block, xr_snd.at[k], xr_rcv.at[k], at_x(1))
        send(block, block, xl_snd.at[k], xl_rcv.at[k], at_x(-1))

    low = total // 2

    def from_x(k):
        left = rows_of(group(k) * NX + (x - 1) % NX)
        remote(left, left, xr_snd.at[k], xr_rcv.at[k], at_x(1)).wait_recv()
        piece = rows_of(group(k) * NX + (x - 1) % NX, 0, low)
        send(piece, piece, fr_snd.at[k], fr_rcv.at[k], at_x(1))
        right = rows_of(group(k) * NX + (x + 1) % NX)
        remote(right, right, xl_snd.at[k], xl_rcv.at[k], at_x(-1)).wait_recv()
        piece = rows_of(group(k) * NX + (x + 1) % NX, low, total - low)
        send(piece, piece, fl_snd.at[k], fl_rcv.at[k], at_x(-1))

    def from_far(k):
        piece = rows_of(group(k) * NX + (x + 2) % NX, 0, low)
        remote(piece, piece, fr_snd.at[k], fr_rcv.at[k], at_x(1)).wait_recv()
        piece = rows_of(group(k) * NX + (x + 2) % NX, low, total - low)
        remote(piece, piece, fl_snd.at[k], fl_rcv.at[k], at_x(-1)).wait_recv()

    def span_of(k):
        return pl.ds(pl.multiple_of(group(k) * span, span), span)

    nt = (((1,), (1,)), ((), ()))

    def multiply(k):
        here = span_of(k)
        acc = jnp.zeros((span, 2 * units), F32)
        for j in range(NZ * planes // 2):
            a, b = 2 * j, 2 * j + 1
            lhs = jnp.concatenate([rows[a, here, :], rows[b, here, :]], axis=1)
            rhs = jnp.concatenate(
                [
                    wcat[a // planes, :, (a % planes) * LANES : (a % planes + 1) * LANES],
                    wcat[b // planes, :, (b % planes) * LANES : (b % planes + 1) * LANES],
                ],
                axis=1,
            )
            acc = acc + lax.dot_general(lhs, rhs, nt, preferred_element_type=F32)
        part[here, :] = acc

    def to_sibling(k):
        here = span_of(k)
        send(part.at[here, :], part_in.at[here, :], p_snd.at[k], p_rcv.at[k], sib)

    partner_tok = (((expert ^ flip) * 2 + (y % 2)) * NX) + x

    def joined(k):
        here = span_of(k)
        remote(part.at[here, :], part_in.at[here, :], p_snd.at[k], p_rcv.at[k], sib).wait_recv()
        both = part[here, :] + part_in[here, :]
        full[here, :] = both
        swap[here, :] = both.astype(BF16)

    def at(off):
        g = (y + off + NY) % NY
        return g, pl.ds(pl.multiple_of(g * span, span), span)

    def swap_copy(off):
        g, here = at(off)
        return remote(swap.at[here, :], swap_in.at[here, :], e_snd.at[g], e_rcv.at[g], (partner_tok, exp))

    def to_partner(k):
        @pl.when(core == 1)
        def _():
            swap_copy(ORDER[k]).start()

    lane = lane[:1]
    zero = jnp.zeros((1, LANES), F32)
    freq_v, label_v = zero, jnp.full((1, LANES), -1, jnp.int32)
    own_label = jnp.int32(0)
    for e in range(EXPERTS):
        freq_v = jnp.where(lane == e, freq[e].astype(F32), freq_v)
        label_v = jnp.where(lane == e, labels[e], label_v)
        own_label = jnp.where(expert == e, labels[e], own_label)
    member = jnp.where(label_v == own_label, 1.0, 0.0).astype(F32)
    member_freq = member * freq_v
    coef = member_freq / jnp.sum(member_freq, axis=1, keepdims=True)
    own_lane = jnp.where(lane == expert, 1.0, 0.0).astype(F32)
    own = jnp.sum(coef * own_lane, axis=1, keepdims=True)
    other = jnp.sum(coef * (1.0 - own_lane), axis=1, keepdims=True)
    taken = jnp.where(core == 1, own * member, own_lane)

    def activate(off):
        g, here = at(off)

        @pl.when(core == 1)
        def _():
            swap_copy(off).wait_recv()
            v = own * full[here, :] + other * swap_in[here, :].astype(F32)
            full[here, :] = v

        v = full[here, :]
        gate, upper = v[:, :units], v[:, units:]
        hid[z, here, :] = (gate / (1.0 + jnp.exp(-gate)) * upper).astype(BF16)

    def along_z(off):
        g, here = at(off)
        for d in (4, 3, 5, 2, 6, 1, 7):
            remote(hid.at[z, here, :], hid.at[z, here, :], h_snd.at[g], h_rcv.at[g], at_z(d)).start()

    def seven(off):
        return hid.at[pl.ds(0, NZ - 1), at(off)[1], :]

    def y_copy(off):
        g, _ = at(off)
        return remote(ysend.at[g], yrecv.at[y], y_snd.at[g], y_rcv.at[y], (g * NX + x, exp))

    def finish(off):
        g, here = at(off)
        pltpu.make_async_copy(seven(off), seven(off), h_rcv.at[g]).wait()
        acc = jnp.zeros((span, 2 * width), F32)
        for j in range(NZ // 2):
            lhs = jnp.concatenate([hid[2 * j, here, :], hid[2 * j + 1, here, :]], axis=1)
            acc = acc + jnp.dot(
                lhs, wd[2 * j * units : 2 * (j + 1) * units, :], preferred_element_type=F32
            )
        weight = jnp.sum(rows[NZ * planes, here, :].astype(F32) * taken, axis=1, keepdims=True)
        acc = acc * weight
        ysend[g] = acc.astype(BF16)

        @pl.when(g == y)
        def _():
            yown[...] = acc

        @pl.when(g != y)
        def _():
            y_copy(off).start()

    if flip == 2:
        pair_order, pair_step = PAIR_ORDER[4]
    else:
        above = (expert % 2 == 0) if flip == 1 else (expert % 2 == 1)
        pair_step = PAIR_ORDER[2][1]
        pair_order = [jnp.where(above, a, b) for a, b in zip(PAIR_ORDER[2][0], PAIR_ORDER[-2][0])]

    def both_cores(action, plain, paired):
        for i in range(max(len(plain), len(paired))):
            if i < len(plain) and i < len(paired):
                action(jnp.where(core == 1, paired[i], plain[i]))
            elif i < len(plain):
                pl.when(core == 0)(functools.partial(action, plain[i]))
            else:
                pl.when(core == 1)(functools.partial(action, paired[i]))

    def due(step):
        plain = [ORDER[k] for k in range(NY) if k + 2 == step]
        return plain, [pair_order[k] for k in range(NY) if pair_step[k] == step]

    along_y(0)
    along_x(0)
    for copy in loads:
        copy.wait()
    ahead = 1
    last = max(pair_step) + LAG
    for k in range(last + 1):
        while ahead < NY and ahead <= k + 2:
            from_y(ahead)
            along_y(ahead)
            along_x(ahead)
            ahead += 1
        if k < NY:
            from_x(k)
        if 0 <= k - 2 < NY:
            joined(k - 2)
        if k == 1:
            for zz in range(NZ):
                for which in range(2):
                    i = 2 * zz + which
                    dst = wcat.at[zz, pl.ds(pl.multiple_of(which * units + (1 - core) * half, half), half), :]
                    remote(dst, dst, w_snd.at[i], w_rcv.at[i], sib).wait_recv()
        if 0 <= k - 1 < NY:
            from_far(k - 1)
            multiply(k - 1)
        if 0 <= k - 2 < NY:
            to_partner(k - 2)
        if k == 2 + LAG:
            theirs = wd.at[:, pl.ds(pl.multiple_of((1 - core) * width, LANES), width)]
            remote(theirs, theirs, w_snd.at[2 * NZ], w_rcv.at[2 * NZ], sib).wait_recv()
        both_cores(finish, *due(k - LAG))
        both_cores(activate, *due(k))
        if 0 <= k - 1 < NY:
            to_sibling(k - 1)
        both_cores(along_z, *due(k))

    acc = yown[...]
    for k in range(1, NY):
        g = (y + k) % NY
        remote(ysend.at[g], yrecv.at[g], y_snd.at[g], y_rcv.at[g], at_y(k)).wait_recv()
        acc = acc + yrecv[g].astype(F32)
    xsend[...] = acc.astype(BF16).reshape(NX, tok_dev, 2 * width)
    yown[...] = acc
    for k in range(1, NX):
        send(xsend.at[(x + k) % NX], xrecv.at[k], x_snd.at[k], x_rcv.at[k], at_x(k))
    acc = yown[pl.ds(pl.multiple_of(x * tok_dev, tok_dev), tok_dev), :]
    for k in range(1, NX):
        remote(xsend.at[0], xrecv.at[k], x_snd.at[k], x_rcv.at[k], at_x(k)).wait_recv()
        acc = acc + xrecv[k].astype(F32)
    kept = jnp.where(core == 0, acc[:, :width], acc[:, width:]).astype(BF16)
    fsend[...] = jnp.where(core == 0, acc[:, width:], acc[:, :width]).astype(BF16)
    send(fsend, frecv, f_snd, f_rcv, sib)
    remote(fsend, frecv, f_snd, f_rcv, sib).wait_recv()
    back = frecv[...]
    first_out[...] = jnp.where(core == 0, kept, back)
    second_out[...] = jnp.where(core == 0, back, kept)

    for copy in zs + gifts + sent:
        copy.wait_send()
    for off in range(NY):
        g, _ = at(off)
        pltpu.make_async_copy(seven(off), seven(off), h_snd.at[g]).wait()
        if off > 0:
            y_copy(off).wait_send()

    @pl.when(core == 1)
    def _():
        for off in range(NY):
            swap_copy(off).wait_send()


def local(tokens, route_ids, gate_codes, merge_labels, freq_counts, w_gate, w_up, w_down):
    tok_dev, width = tokens.shape
    half = w_gate.shape[0]
    count, depth = NX * NY * tok_dev, w_down.shape[0]
    units = 2 * half
    planes = width // LANES
    span = NX * tok_dev
    dma = pltpu.SemaphoreType.DMA
    scratch = [
        pltpu.VMEM((NZ * planes + 1, count, LANES), BF16),
        pltpu.VMEM((NZ, 2 * units, width), BF16),
        pltpu.VMEM((depth, 2 * width), BF16),
        pltpu.VMEM((count, 2 * units), F32),
        pltpu.VMEM((count, 2 * units), F32),
        pltpu.VMEM((count, 2 * units), F32),
        pltpu.VMEM((count, 2 * units), BF16),
        pltpu.VMEM((count, 2 * units), BF16),
        pltpu.VMEM((NZ, count, units), BF16),
        pltpu.VMEM((NY, span, 2 * width), BF16),
        pltpu.VMEM((NY, span, 2 * width), BF16),
        pltpu.VMEM((span, 2 * width), F32),
        pltpu.VMEM((NX, tok_dev, 2 * width), BF16),
        pltpu.VMEM((NX, tok_dev, 2 * width), BF16),
        pltpu.VMEM((tok_dev, width), BF16),
        pltpu.VMEM((tok_dev, width), BF16),
        dma((planes,)),
        dma((2 * NZ + 1,)),
        dma((2 * NZ + 1,)),
        dma((2 * NZ + 1,)),
        dma((NZ,)),
        dma((NZ,)),
        *[dma((NY // 2,))] * 4,
        *[dma((NY,))] * 16,
        dma((NX,)),
        dma((NX,)),
        dma(()),
        dma(()),
    ]
    smem, hbm = pl.BlockSpec(memory_space=pltpu.SMEM), pl.BlockSpec(memory_space=pl.ANY)
    vmem = pl.BlockSpec(memory_space=pltpu.VMEM)
    out = jax.ShapeDtypeStruct((tok_dev, width), BF16)

    def variant(flip):
        def run(*args):
            return pl.pallas_call(
                functools.partial(kernel, flip),
                out_shape=(out, out),
                in_specs=[smem, smem, vmem, vmem, hbm, hbm, hbm, hbm],
                out_specs=(vmem, vmem),
                scratch_shapes=scratch,
                compiler_params=pltpu.CompilerParams(
                    collective_id=flip, has_side_effects=True, vmem_limit_bytes=60 * 1024 * 1024
                ),
                name=f"layer_flip{flip}",
            )(*args)

        return run

    zero, one, two = (merge_labels[e] for e in range(3))
    pairing = jnp.where(one == zero, 0, jnp.where(two == zero, 1, 2))
    return lax.switch(
        pairing,
        [variant(1), variant(2), variant(3)],
        merge_labels, freq_counts, route_ids.T, gate_codes.T, tokens, w_gate, w_up, w_down,
    )


def solution(mesh):
    return jax.shard_map(
        local,
        mesh=mesh,
        in_specs=(
            P("tok", "exp"),
            P("tok", None),
            P("tok", None),
            P(),
            P(),
            P(("tok", "exp"), None),
            P(("tok", "exp"), None),
            P("tok", "exp"),
        ),
        out_specs=(P("tok", "exp"), P("tok", "exp")),
        check_vma=False,
    )
```

```python
import functools

import jax
import jax.numpy as jnp
from jax import lax
from jax.experimental import pallas as pl
from jax.experimental.pallas import tpu as pltpu
from jax.sharding import PartitionSpec as P

EXPERTS = 4
LANES = 128
NX, NY, NZ = 4, 8, 8
MESH = pl.DeviceIdType.MESH
BF16, F32 = jnp.bfloat16, jnp.float32
UP_STEPS, DOWN_STEPS = 3, 4
SIDE = 2
PLAIN = {
    2: (0, 1, 2, -1, 3, -2, -4, -3),
    -2: (0, -1, -2, 1, -3, 2, -4, 3),
    4: (0, 1, 2, -2, -1, -3, 3, -4),
    -4: (0, -1, -2, 2, 1, 3, -3, -4),
}
PAIRED = {
    2: (1, 0, 2, -1, 3, -2, -4, -3),
    -2: (-1, -2, 0, -3, 1, -4, 2, 3),
    4: (2, -2, -1, -3, 1, 3, 0, -4),
    -4: (-2, 2, 3, 1, -3, -1, -4, 0),
}
READY = {2: (1, 2, 2, 4, 4, 6, 6, 7), 4: (2, 3, 5, 5, 6, 6, 7, 7)}
HOPS = {d: tuple(abs(o) for o in PLAIN[d]) for d in (2, 4)}
LAG, SUM_LAG = 3, 2


def kernel(
    flip, labels_hbm, freq_hbm, ids_hbm, codes_hbm, tokens, w_gate, w_up, w_down, first_out, second_out,
    labels, freq, ids, codes,
    rows, wcat, wd, part, part_in, full, swap, swap_in, hid, xsend, xrecv, xown, acc_mine, ysend, yrecv, fsend, frecv,
    s_loc, t_loc, w_loc, w_snd, w_rcv, z_snd, z_rcv, up_snd, up_rcv, dn_snd, dn_rcv,
    xr_snd, xr_rcv, xl_snd, xl_rcv, fr_snd, fr_rcv, fl_snd, fl_rcv,
    p_snd, p_rcv, e_snd, e_rcv, h_snd, h_rcv, y_snd, y_rcv, x_snd, x_rcv, f_snd, f_rcv, su_snd, su_rcv, sd_snd, sd_rcv,
):
    tok, exp = lax.axis_index("tok"), lax.axis_index("exp")
    y, x = tok // NX, tok % NX
    z, core = exp // 2, exp % 2
    sib = (tok, z * 2 + (1 - core))
    half = w_gate.shape[0]
    units = 2 * half
    tok_dev, width = tokens.shape
    planes = width // LANES
    total = NZ * planes + 1
    span = NX * tok_dev
    expert = y // 2

    def at_z(k):
        return (tok, ((z + k) % NZ) * 2 + core)

    def at_y(k):
        return (((y + k) % NY) * NX + x, exp)

    def at_x(k):
        return (y * NX + (x + k) % NX, exp)

    def remote(src, dst, snd, rcv, dev):
        return pltpu.make_async_remote_copy(
            src_ref=src, dst_ref=dst, send_sem=snd, recv_sem=rcv, device_id=dev, device_id_type=MESH
        )

    def rows_of(t, lo=0, n=None):
        n = total if n is None else n
        return rows.at[pl.ds(lo, n), pl.ds(pl.multiple_of(t * tok_dev, tok_dev), tok_dev), :]

    barrier = pltpu.get_barrier_semaphore()
    greeted = [at_z(k) for k in range(1, NZ)] + [at_y(k) for k in range(1, NY)]
    greeted += [at_x(k) for k in range(1, NX)] + [sib]
    for dev in greeted:
        pl.semaphore_signal(barrier, inc=1, device_id=dev, device_id_type=MESH)

    mine = pl.ds(pl.multiple_of(tok * tok_dev, tok_dev), tok_dev)
    locals_ = []
    for i in range(planes):
        locals_.append(
            pltpu.make_async_copy(
                tokens.at[:, pl.ds(i * LANES, LANES)], rows.at[z * planes + i, mine, :], t_loc.at[i]
            )
        )
    for copy in locals_:
        copy.start()

    small = []
    for i, (src, dst) in enumerate(((ids_hbm, ids), (codes_hbm, codes), (labels_hbm, labels), (freq_hbm, freq))):
        small.append(pltpu.make_async_copy(src, dst, s_loc.at[i]))
    for copy in small:
        copy.start()

    loads = []
    for zz in range(NZ):
        for which, ref in enumerate((w_gate, w_up)):
            dst = wcat.at[zz, pl.ds(pl.multiple_of(which * units + core * half, half), half), :]
            cols = pl.ds(pl.multiple_of((2 * zz + core) * width, LANES), width)
            loads.append(pltpu.make_async_copy(ref.at[:, cols], dst, w_loc.at[2 * zz + which]))
    wide = pl.ds(pl.multiple_of(core * width, LANES), width)
    loads.append(pltpu.make_async_copy(w_down, wd.at[:, wide], w_loc.at[2 * NZ]))
    for copy in loads:
        copy.start()
    for copy in small:
        copy.wait()
    lane = lax.broadcasted_iota(jnp.int32, (tok_dev, LANES), 1)
    diag = lax.broadcasted_iota(jnp.int32, (tok_dev, tok_dev), 0) == lax.broadcasted_iota(
        jnp.int32, (tok_dev, tok_dev), 1
    )
    share = jnp.zeros((tok_dev, LANES), F32)
    for e in range(EXPERTS):
        line = jnp.sum(jnp.where(ids[...] == e, codes[...].astype(F32) / 256.0, 0.0), axis=0, keepdims=True)
        column = jnp.sum(jnp.where(diag, jnp.broadcast_to(line, diag.shape), 0.0), axis=1, keepdims=True)
        share = share + jnp.where(lane == e, column, 0.0)
    rows[NZ * planes, mine, :] = share.astype(BF16)

    for copy in locals_:
        copy.wait()
    pl.semaphore_wait(barrier, len(greeted))

    zs = []
    own_planes = rows.at[pl.ds(z * planes, planes), mine, :]
    for k in (1, 7, 2, 6, 3, 5, 4):
        zs.append(remote(own_planes, own_planes, z_snd.at[k], z_rcv.at[k], at_z(k)))
    for copy in zs:
        copy.start()

    gifts = []
    for zz in range(NZ):
        for which, ref in enumerate((w_gate, w_up)):
            dst = wcat.at[zz, pl.ds(pl.multiple_of(which * units + core * half, half), half), :]
            cols = pl.ds(pl.multiple_of((2 * zz + (1 - core)) * width, LANES), width)
            i = 2 * zz + which
            gifts.append(remote(ref.at[:, cols], dst, w_snd.at[i], w_rcv.at[i], sib))
    gifts.append(remote(w_down, wd.at[:, wide], w_snd.at[2 * NZ], w_rcv.at[2 * NZ], sib))
    for copy in gifts:
        copy.start()

    if flip == 2:
        above, far = expert < EXPERTS // 2, 4
    else:
        above, far = (expert % 2 == 0) if flip == 1 else (expert % 2 == 1), 2
    plain_order = [jnp.where(above, a, b) for a, b in zip(PLAIN[far], PLAIN[-far])]
    pair_order = [jnp.where(above, a, b) for a, b in zip(PAIRED[far], PAIRED[-far])]
    pair_step = [r + 3 for r in READY[far]]

    def group(k):
        return (y + plain_order[k] + NY) % NY

    sent = []

    def send(*args):
        copy = remote(*args)
        copy.start()
        sent.append(copy)

    side = SIDE * planes
    main = total - side

    def spread(piece, with_y):
        for snd, rcv, dev in ((xr_snd, xr_rcv, at_x(1)), (xl_snd, xl_rcv, at_x(-1))):
            remote(piece, piece, snd.at[0], rcv.at[0], dev).start()

        @pl.when(with_y)
        def _():
            for snd, rcv, dev in ((up_snd, up_rcv, at_y(1)), (dn_snd, dn_rcv, at_y(-1))):
                remote(piece, piece, snd.at[0], rcv.at[0], dev).start()

    def along_y(hop):
        if hop < UP_STEPS:
            block = rows_of(((y - hop + NY) % NY) * NX + x, side, main)
            send(block, block, up_snd.at[hop], up_rcv.at[hop], at_y(1))
        if hop < DOWN_STEPS:
            block = rows_of(((y + hop) % NY) * NX + x, side, main)
            send(block, block, dn_snd.at[hop], dn_rcv.at[hop], at_y(-1))

    def from_y(hop):
        if hop <= UP_STEPS:
            block = rows_of(((y - hop + NY) % NY) * NX + x, side, main)
            remote(block, block, up_snd.at[hop - 1], up_rcv.at[hop - 1], at_y(1)).wait_recv()
        if hop <= DOWN_STEPS:
            block = rows_of(((y + hop) % NY) * NX + x, side, main)
            remote(block, block, dn_snd.at[hop - 1], dn_rcv.at[hop - 1], at_y(-1)).wait_recv()

    def planes_of(k):
        return (0, total) if k == 0 else (side, main)

    def along_x(k):
        block = rows_of(group(k) * NX + x, *planes_of(k))
        send(block, block, xr_snd.at[k], xr_rcv.at[k], at_x(1))
        send(block, block, xl_snd.at[k], xl_rcv.at[k], at_x(-1))

    def pieces(k, t):
        lo, n = planes_of(k)
        return rows_of(t, lo, n // 2), rows_of(t, lo + n // 2, n - n // 2)

    def from_x(k):
        left, right = group(k) * NX + (x + NX - 1) % NX, group(k) * NX + (x + 1) % NX
        block = rows_of(left, *planes_of(k))
        remote(block, block, xr_snd.at[k], xr_rcv.at[k], at_x(1)).wait_recv()
        piece = pieces(k, left)[0]
        send(piece, piece, fr_snd.at[k], fr_rcv.at[k], at_x(1))
        block = rows_of(right, *planes_of(k))
        remote(block, block, xl_snd.at[k], xl_rcv.at[k], at_x(-1)).wait_recv()
        piece = pieces(k, right)[1]
        send(piece, piece, fl_snd.at[k], fl_rcv.at[k], at_x(-1))

    def from_far(k):
        low, high = pieces(k, group(k) * NX + (x + 2) % NX)
        remote(low, low, fr_snd.at[k], fr_rcv.at[k], at_x(1)).wait_recv()
        remote(high, high, fl_snd.at[k], fl_rcv.at[k], at_x(-1)).wait_recv()

    def side_block(g):
        return rows.at[pl.ds(0, side), pl.ds(pl.multiple_of(g * span, span), span), :]

    def side_on(hop):
        if hop < DOWN_STEPS:
            block = side_block((y + hop) % NY)
            send(block, block, sd_snd.at[hop], sd_rcv.at[hop], at_y(-1))
        if hop < UP_STEPS:
            block = side_block((y - hop + NY) % NY)
            send(block, block, su_snd.at[hop], su_rcv.at[hop], at_y(1))

    def side_in(hop):
        if hop <= UP_STEPS:
            block = side_block((y - hop + NY) % NY)
            remote(block, block, su_snd.at[hop - 1], su_rcv.at[hop - 1], at_y(1)).wait_recv()
        if hop <= DOWN_STEPS:
            block = side_block((y + hop) % NY)
            remote(block, block, sd_snd.at[hop - 1], sd_rcv.at[hop - 1], at_y(-1)).wait_recv()

    def span_of(k):
        return pl.ds(pl.multiple_of(group(k) * span, span), span)

    nt = (((1,), (1,)), ((), ()))

    def multiply(k):
        here = span_of(k)
        acc = jnp.zeros((span, 2 * units), F32)
        for j in range(NZ * planes // 2):
            a, b = 2 * j, 2 * j + 1
            lhs = jnp.concatenate([rows[a, here, :], rows[b, here, :]], axis=1)
            rhs = jnp.concatenate(
                [
                    wcat[a // planes, :, (a % planes) * LANES : (a % planes + 1) * LANES],
                    wcat[b // planes, :, (b % planes) * LANES : (b % planes + 1) * LANES],
                ],
                axis=1,
            )
            acc = acc + lax.dot_general(lhs, rhs, nt, preferred_element_type=F32)
        part[here, :] = acc

    def to_sibling(k):
        here = span_of(k)
        send(part.at[here, :], part_in.at[here, :], p_snd.at[k], p_rcv.at[k], sib)

    partner_tok = (((expert ^ flip) * 2 + (y % 2)) * NX) + x

    def joined(k):
        here = span_of(k)
        remote(part.at[here, :], part_in.at[here, :], p_snd.at[k], p_rcv.at[k], sib).wait_recv()
        both = part[here, :] + part_in[here, :]
        full[here, :] = both
        swap[here, :] = both.astype(BF16)

    def at(off):
        g = (y + off + NY) % NY
        return g, pl.ds(pl.multiple_of(g * span, span), span)

    def swap_copy(off):
        g, here = at(off)
        return remote(swap.at[here, :], swap_in.at[here, :], e_snd.at[g], e_rcv.at[g], (partner_tok, exp))

    def to_partner(k):
        @pl.when(core == 1)
        def _():
            swap_copy(plain_order[k]).start()

    lane = lane[:1]
    zero = jnp.zeros((1, LANES), F32)
    freq_v, label_v = zero, jnp.full((1, LANES), -1, jnp.int32)
    own_label = jnp.int32(0)
    for e in range(EXPERTS):
        freq_v = jnp.where(lane == e, freq[e].astype(F32), freq_v)
        label_v = jnp.where(lane == e, labels[e], label_v)
        own_label = jnp.where(expert == e, labels[e], own_label)
    member = jnp.where(label_v == own_label, 1.0, 0.0).astype(F32)
    member_freq = member * freq_v
    coef = member_freq / jnp.sum(member_freq, axis=1, keepdims=True)
    own_lane = jnp.where(lane == expert, 1.0, 0.0).astype(F32)
    own = jnp.sum(coef * own_lane, axis=1, keepdims=True)
    other = jnp.sum(coef * (1.0 - own_lane), axis=1, keepdims=True)
    taken = jnp.where(core == 1, own * member, own_lane)

    def activate(off):
        g, here = at(off)

        @pl.when(core == 1)
        def _():
            swap_copy(off).wait_recv()
            v = own * full[here, :] + other * swap_in[here, :].astype(F32)
            full[here, :] = v

        v = full[here, :]
        gate, upper = v[:, :units], v[:, units:]
        hid[z, here, :] = (gate / (1.0 + jnp.exp(-gate)) * upper).astype(BF16)

    def along_z(off):
        g, here = at(off)
        for d in (4, 3, 5, 2, 6, 1, 7):
            remote(hid.at[z, here, :], hid.at[z, here, :], h_snd.at[g], h_rcv.at[g], at_z(d)).start()

    def seven(off):
        return hid.at[pl.ds(0, NZ - 1), at(off)[1], :]

    def x_copy(off, d):
        g, _ = at(off)
        there = (x + d) % NX
        part_rows = pl.ds(pl.multiple_of(there * tok_dev, tok_dev), tok_dev)
        return remote(xsend.at[g, part_rows, :], xrecv.at[g, NX - d], x_snd.at[g], x_rcv.at[g], at_x(d))

    def three(off):
        return xrecv.at[at(off)[0], pl.ds(1, NX - 1)]

    def y_copy(off):
        g, _ = at(off)
        return remote(ysend.at[g], yrecv.at[y], y_snd.at[g], y_rcv.at[y], (g * NX + x, exp))

    def finish(off):
        g, here = at(off)
        pltpu.make_async_copy(seven(off), seven(off), h_rcv.at[g]).wait()
        acc = jnp.zeros((span, 2 * width), F32)
        for j in range(NZ // 2):
            lhs = jnp.concatenate([hid[2 * j, here, :], hid[2 * j + 1, here, :]], axis=1)
            acc = acc + jnp.dot(
                lhs, wd[2 * j * units : 2 * (j + 1) * units, :], preferred_element_type=F32
            )
        weight = jnp.sum(rows[NZ * planes, here, :].astype(F32) * taken, axis=1, keepdims=True)
        acc = acc * weight
        xsend[g] = acc.astype(BF16)
        acc_mine[...] = acc
        xown[g] = acc_mine[pl.ds(pl.multiple_of(x * tok_dev, tok_dev), tok_dev), :]
        for d in (2, 1, 3):
            x_copy(off, d).start()

    def reduce(off):
        g, _ = at(off)
        pltpu.make_async_copy(three(off), three(off), x_rcv.at[g]).wait()
        acc = xown[g]
        for d in range(1, NX):
            acc = acc + xrecv[g, d].astype(F32)
        xown[g] = acc
        ysend[g] = acc.astype(BF16)

        @pl.when(g != y)
        def _():
            y_copy(off).start()

    def both_cores(action, plain, paired):
        for i in range(max(len(plain), len(paired))):
            if i < len(plain) and i < len(paired):
                action(jnp.where(core == 1, paired[i], plain[i]))
            elif i < len(plain):
                pl.when(core == 0)(functools.partial(action, plain[i]))
            else:
                pl.when(core == 1)(functools.partial(action, paired[i]))

    def due(step):
        plain = [plain_order[k] for k in range(NY) if k + 2 == step]
        return plain, [pair_order[k] for k in range(NY) if pair_step[k] == step]

    spread(rows.at[pl.ds(NZ * planes, 1), mine, :], tok >= 0)
    spread(own_planes, z >= SIDE)
    for k in (1, 7, 2, 6, 3, 5, 4):
        zz = (z - k + NZ) % NZ
        got = rows.at[pl.ds(zz * planes, planes), mine, :]
        remote(got, got, z_snd.at[k], z_rcv.at[k], at_z(k)).wait_recv()
        spread(got, zz >= SIDE)
    block = rows_of(tok)
    sent.append(remote(block, block, xr_snd.at[0], xr_rcv.at[0], at_x(1)))
    sent.append(remote(block, block, xl_snd.at[0], xl_rcv.at[0], at_x(-1)))
    block = rows_of(tok, side, main)
    sent.append(remote(block, block, up_snd.at[0], up_rcv.at[0], at_y(1)))
    sent.append(remote(block, block, dn_snd.at[0], dn_rcv.at[0], at_y(-1)))
    for copy in loads:
        copy.wait()
    ahead = 1
    hops = NY // 2
    last = max(pair_step) + LAG + SUM_LAG
    for k in range(last + 1):
        late = k > NY
        if k + 1 <= hops:
            from_y(k + 1)
            along_y(k + 1)
        while ahead < NY and ahead <= k + 2 and HOPS[far][ahead] <= k + 1:
            along_x(ahead)
            ahead += 1
        if 0 <= k - 2 < NY:
            joined(k - 2)
        if k == 2 + LAG:
            theirs = wd.at[:, pl.ds(pl.multiple_of((1 - core) * width, LANES), width)]
            remote(theirs, theirs, w_snd.at[2 * NZ], w_rcv.at[2 * NZ], sib).wait_recv()
        if not late:
            both_cores(reduce, *due(k - LAG - SUM_LAG))
            both_cores(finish, *due(k - LAG))
        if 0 <= k - 2 < NY:
            to_partner(k - 2)
        both_cores(activate, *due(k))
        if k < NY:
            from_x(k)
        both_cores(along_z, *due(k))
        if k == 1:
            for zz in range(NZ):
                for which in range(2):
                    i = 2 * zz + which
                    dst = wcat.at[zz, pl.ds(pl.multiple_of(which * units + (1 - core) * half, half), half), :]
                    remote(dst, dst, w_snd.at[i], w_rcv.at[i], sib).wait_recv()
        if 0 <= k - 1 < NY:
            from_far(k - 1)
            if k == 1:
                side_on(0)
            elif k - 1 <= hops:
                side_in(k - 1)
                side_on(k - 1)
            multiply(k - 1)
            to_sibling(k - 1)
        if late:
            both_cores(finish, *due(k - LAG))
            both_cores(reduce, *due(k - LAG - SUM_LAG))

    acc = xown[y]
    for k in range(1, NY):
        g = (y + k) % NY
        remote(ysend.at[g], yrecv.at[g], y_snd.at[g], y_rcv.at[g], at_y(k)).wait_recv()
        acc = acc + yrecv[g].astype(F32)
    kept = jnp.where(core == 0, acc[:, :width], acc[:, width:]).astype(BF16)
    fsend[...] = jnp.where(core == 0, acc[:, width:], acc[:, :width]).astype(BF16)
    send(fsend, frecv, f_snd, f_rcv, sib)
    remote(fsend, frecv, f_snd, f_rcv, sib).wait_recv()
    back = frecv[...]
    first_out[...] = jnp.where(core == 0, kept, back)
    second_out[...] = jnp.where(core == 0, back, kept)

    for copy in zs + gifts + sent:
        copy.wait_send()
    for off in range(NY):
        g, _ = at(off)
        pltpu.make_async_copy(seven(off), seven(off), h_snd.at[g]).wait()
        pltpu.make_async_copy(three(off), three(off), x_snd.at[g]).wait()
        if off > 0:
            y_copy(off).wait_send()

    @pl.when(core == 1)
    def _():
        for off in range(NY):
            swap_copy(off).wait_send()


def local(tokens, route_ids, gate_codes, merge_labels, freq_counts, w_gate, w_up, w_down):
    tok_dev, width = tokens.shape
    half = w_gate.shape[0]
    count, depth = NX * NY * tok_dev, w_down.shape[0]
    units = 2 * half
    planes = width // LANES
    span = NX * tok_dev
    dma = pltpu.SemaphoreType.DMA
    ids_shape = route_ids.shape[::-1]
    scratch = [
        pltpu.SMEM((EXPERTS,), jnp.int32),
        pltpu.SMEM((EXPERTS,), jnp.int32),
        pltpu.VMEM(ids_shape, jnp.int32),
        pltpu.VMEM(ids_shape, jnp.int32),
        pltpu.VMEM((NZ * planes + 1, count, LANES), BF16),
        pltpu.VMEM((NZ, 2 * units, width), BF16),
        pltpu.VMEM((depth, 2 * width), BF16),
        pltpu.VMEM((count, 2 * units), F32),
        pltpu.VMEM((count, 2 * units), F32),
        pltpu.VMEM((count, 2 * units), F32),
        pltpu.VMEM((count, 2 * units), BF16),
        pltpu.VMEM((count, 2 * units), BF16),
        pltpu.VMEM((NZ, count, units), BF16),
        pltpu.VMEM((NY, span, 2 * width), BF16),
        pltpu.VMEM((NY, NX, tok_dev, 2 * width), BF16),
        pltpu.VMEM((NY, tok_dev, 2 * width), F32),
        pltpu.VMEM((span, 2 * width), F32),
        pltpu.VMEM((NY, tok_dev, 2 * width), BF16),
        pltpu.VMEM((NY, tok_dev, 2 * width), BF16),
        pltpu.VMEM((tok_dev, width), BF16),
        pltpu.VMEM((tok_dev, width), BF16),
        dma((4,)),
        dma((planes,)),
        dma((2 * NZ + 1,)),
        dma((2 * NZ + 1,)),
        dma((2 * NZ + 1,)),
        dma((NZ,)),
        dma((NZ,)),
        *[dma((NY // 2,))] * 4,
        *[dma((NY,))] * 16,
        dma((NY,)),
        dma((NY,)),
        dma(()),
        dma(()),
        *[dma((NY // 2,))] * 4,
    ]
    hbm = pl.BlockSpec(memory_space=pltpu.HBM)
    vmem = pl.BlockSpec(memory_space=pltpu.VMEM)
    out = jax.ShapeDtypeStruct((tok_dev, width), BF16)

    def variant(flip):
        def run(*args):
            return pl.pallas_call(
                functools.partial(kernel, flip),
                out_shape=(out, out),
                in_specs=[hbm] * 8,
                out_specs=(vmem, vmem),
                scratch_shapes=scratch,
                compiler_params=pltpu.CompilerParams(
                    collective_id=flip, has_side_effects=True, vmem_limit_bytes=60 * 1024 * 1024
                ),
                name=f"layer_flip{flip}",
            )(*args)

        return run

    spot = jnp.maximum(jnp.arange(EXPERTS, dtype=jnp.int32) - 1, 0)
    pairing = jnp.sum(jnp.where(merge_labels == merge_labels[0], spot, 0))
    return lax.switch(
        pairing,
        [variant(1), variant(2), variant(3)],
        merge_labels, freq_counts, route_ids.T, gate_codes.T, tokens, w_gate, w_up, w_down,
    )


def solution(mesh):
    return jax.shard_map(
        local,
        mesh=mesh,
        in_specs=(
            P("tok", "exp"),
            P("tok", None),
            P("tok", None),
            P(),
            P(),
            P(("tok", "exp"), None),
            P(("tok", "exp"), None),
            P("tok", "exp"),
        ),
        out_specs=(P("tok", "exp"), P("tok", "exp")),
        check_vma=False,
    )
```

```python
import functools

import jax
import jax.numpy as jnp
from jax import lax
from jax.experimental import pallas as pl
from jax.experimental.pallas import tpu as pltpu
from jax.sharding import PartitionSpec as P

EXPERTS = 4
LANES = 128
NX, NY, NZ = 4, 8, 8
MESH = pl.DeviceIdType.MESH
BF16, F32 = jnp.bfloat16, jnp.float32
UP_STEPS, DOWN_STEPS = 4, 3
SIDE = 1
PLAIN = {
    2: (0, 1, 2, -1, 3, -2, -4, -3),
    -2: (0, -1, -2, 1, -3, 2, -4, 3),
    4: (0, 1, 2, -2, -1, -3, 3, -4),
    -4: (0, -1, -2, 2, 1, 3, -3, -4),
}
PAIRED = {
    2: (1, 0, 2, -1, 3, -2, -4, -3),
    -2: (-1, -2, 0, -3, 1, -4, 2, 3),
    4: (2, -2, -1, -3, 1, 3, 0, -4),
    -4: (-2, 2, 3, 1, -3, -1, -4, 0),
}
READY = {2: (1, 2, 2, 4, 4, 6, 6, 7), 4: (2, 3, 5, 5, 6, 6, 7, 7)}
HOPS = {d: tuple(abs(o) for o in PLAIN[d]) for d in (2, 4)}
LAG, SUM_LAG = 3, 2


def kernel(
    flip, labels_hbm, freq_hbm, ids_hbm, codes_hbm, tokens, w_gate, w_up, w_down, first_out, second_out,
    labels, freq, ids, codes,
    rows, wcat, wd, part, part_in, full, swap, swap_in, hid, xsend, xrecv, xown, acc_mine, ysend, yrecv, fsend, frecv,
    s_loc, t_loc, w_loc, w_snd, w_rcv, z_snd, z_rcv, up_snd, up_rcv, dn_snd, dn_rcv,
    xr_snd, xr_rcv, xl_snd, xl_rcv, fr_snd, fr_rcv, fl_snd, fl_rcv,
    p_snd, p_rcv, e_snd, e_rcv, h_snd, h_rcv, y_snd, y_rcv, x_snd, x_rcv, f_snd, f_rcv, su_snd, su_rcv, sd_snd, sd_rcv,
):
    tok, exp = lax.axis_index("tok"), lax.axis_index("exp")
    y, x = tok // NX, tok % NX
    z, core = exp // 2, exp % 2
    sib = (tok, z * 2 + (1 - core))
    half = w_gate.shape[0]
    units = 2 * half
    tok_dev, width = tokens.shape
    planes = width // LANES
    total = NZ * planes + 1
    span = NX * tok_dev
    expert = y // 2

    def at_z(k):
        return (tok, ((z + k) % NZ) * 2 + core)

    def at_y(k):
        return (((y + k) % NY) * NX + x, exp)

    def at_x(k):
        return (y * NX + (x + k) % NX, exp)

    def remote(src, dst, snd, rcv, dev):
        return pltpu.make_async_remote_copy(
            src_ref=src, dst_ref=dst, send_sem=snd, recv_sem=rcv, device_id=dev, device_id_type=MESH
        )

    def rows_of(t, lo=0, n=None):
        n = total if n is None else n
        return rows.at[pl.ds(lo, n), pl.ds(pl.multiple_of(t * tok_dev, tok_dev), tok_dev), :]

    barrier = pltpu.get_barrier_semaphore()
    greeted = [at_z(k) for k in range(1, NZ)] + [at_y(k) for k in range(1, NY)]
    greeted += [at_x(k) for k in range(1, NX)] + [sib]
    for dev in greeted:
        pl.semaphore_signal(barrier, inc=1, device_id=dev, device_id_type=MESH)

    mine = pl.ds(pl.multiple_of(tok * tok_dev, tok_dev), tok_dev)
    locals_ = []
    for i in range(planes):
        locals_.append(
            pltpu.make_async_copy(
                tokens.at[:, pl.ds(i * LANES, LANES)], rows.at[z * planes + i, mine, :], t_loc.at[i]
            )
        )
    for copy in locals_:
        copy.start()

    small = []
    for i, (src, dst) in enumerate(((ids_hbm, ids), (codes_hbm, codes), (labels_hbm, labels), (freq_hbm, freq))):
        small.append(pltpu.make_async_copy(src, dst, s_loc.at[i]))
    for copy in small:
        copy.start()

    for copy in locals_:
        copy.wait()
    pl.semaphore_wait(barrier, len(greeted))

    zs = []
    own_planes = rows.at[pl.ds(z * planes, planes), mine, :]
    for k in (4, 3, 5, 2, 6, 1, 7):
        zs.append(remote(own_planes, own_planes, z_snd.at[k], z_rcv.at[k], at_z(k)))
    for copy in zs:
        copy.start()

    loads = []
    for zz in range(NZ):
        for which, ref in enumerate((w_gate, w_up)):
            dst = wcat.at[zz, pl.ds(pl.multiple_of(which * units + core * half, half), half), :]
            cols = pl.ds(pl.multiple_of((2 * zz + core) * width, LANES), width)
            loads.append(pltpu.make_async_copy(ref.at[:, cols], dst, w_loc.at[2 * zz + which]))
    wide = pl.ds(pl.multiple_of(core * width, LANES), width)
    loads.append(pltpu.make_async_copy(w_down, wd.at[:, wide], w_loc.at[2 * NZ]))
    for copy in loads:
        copy.start()
    gifts = []
    for zz in range(NZ):
        for which, ref in enumerate((w_gate, w_up)):
            dst = wcat.at[zz, pl.ds(pl.multiple_of(which * units + core * half, half), half), :]
            cols = pl.ds(pl.multiple_of((2 * zz + (1 - core)) * width, LANES), width)
            i = 2 * zz + which
            gifts.append(remote(ref.at[:, cols], dst, w_snd.at[i], w_rcv.at[i], sib))
    gifts.append(remote(w_down, wd.at[:, wide], w_snd.at[2 * NZ], w_rcv.at[2 * NZ], sib))
    for copy in gifts:
        copy.start()

    for copy in small:
        copy.wait()
    lane = lax.broadcasted_iota(jnp.int32, (tok_dev, LANES), 1)
    diag = lax.broadcasted_iota(jnp.int32, (tok_dev, tok_dev), 0) == lax.broadcasted_iota(
        jnp.int32, (tok_dev, tok_dev), 1
    )
    share = jnp.zeros((tok_dev, LANES), F32)
    for e in range(EXPERTS):
        line = jnp.sum(jnp.where(ids[...] == e, codes[...].astype(F32) / 256.0, 0.0), axis=0, keepdims=True)
        column = jnp.sum(jnp.where(diag, jnp.broadcast_to(line, diag.shape), 0.0), axis=1, keepdims=True)
        share = share + jnp.where(lane == e, column, 0.0)
    rows[NZ * planes, mine, :] = share.astype(BF16)

    if flip == 2:
        above, far = expert < EXPERTS // 2, 4
    else:
        above, far = (expert % 2 == 0) if flip == 1 else (expert % 2 == 1), 2
    plain_order = [jnp.where(above, a, b) for a, b in zip(PLAIN[far], PLAIN[-far])]
    pair_order = [jnp.where(above, a, b) for a, b in zip(PAIRED[far], PAIRED[-far])]
    pair_step = [r + 3 for r in READY[far]]

    def group(k):
        return (y + plain_order[k] + NY) % NY

    sent = []

    def send(*args):
        copy = remote(*args)
        copy.start()
        sent.append(copy)

    side = SIDE * planes
    main = total - side

    def spread(piece, with_y):
        for snd, rcv, dev in ((xr_snd, xr_rcv, at_x(1)), (xl_snd, xl_rcv, at_x(-1))):
            remote(piece, piece, snd.at[0], rcv.at[0], dev).start()

        @pl.when(with_y)
        def _():
            for snd, rcv, dev in ((up_snd, up_rcv, at_y(1)), (dn_snd, dn_rcv, at_y(-1))):
                remote(piece, piece, snd.at[0], rcv.at[0], dev).start()

    def along_y(hop):
        if hop < UP_STEPS:
            block = rows_of(((y - hop + NY) % NY) * NX + x, side, main)
            send(block, block, up_snd.at[hop], up_rcv.at[hop], at_y(1))
        if hop < DOWN_STEPS:
            block = rows_of(((y + hop) % NY) * NX + x, side, main)
            send(block, block, dn_snd.at[hop], dn_rcv.at[hop], at_y(-1))

    def from_y(hop):
        if hop <= UP_STEPS:
            block = rows_of(((y - hop + NY) % NY) * NX + x, side, main)
            remote(block, block, up_snd.at[hop - 1], up_rcv.at[hop - 1], at_y(1)).wait_recv()
        if hop <= DOWN_STEPS:
            block = rows_of(((y + hop) % NY) * NX + x, side, main)
            remote(block, block, dn_snd.at[hop - 1], dn_rcv.at[hop - 1], at_y(-1)).wait_recv()

    def planes_of(k):
        return (0, total) if k == 0 else (side, main)

    def along_x(k):
        block = rows_of(group(k) * NX + x, *planes_of(k))
        send(block, block, xr_snd.at[k], xr_rcv.at[k], at_x(1))
        send(block, block, xl_snd.at[k], xl_rcv.at[k], at_x(-1))

    def pieces(k, t):
        lo, n = planes_of(k)
        return rows_of(t, lo, n // 2), rows_of(t, lo + n // 2, n - n // 2)

    def from_x(k):
        left, right = group(k) * NX + (x + NX - 1) % NX, group(k) * NX + (x + 1) % NX
        block = rows_of(left, *planes_of(k))
        remote(block, block, xr_snd.at[k], xr_rcv.at[k], at_x(1)).wait_recv()
        piece = pieces(k, left)[0]
        send(piece, piece, fr_snd.at[k], fr_rcv.at[k], at_x(1))
        block = rows_of(right, *planes_of(k))
        remote(block, block, xl_snd.at[k], xl_rcv.at[k], at_x(-1)).wait_recv()
        piece = pieces(k, right)[1]
        send(piece, piece, fl_snd.at[k], fl_rcv.at[k], at_x(-1))

    def from_far(k):
        low, high = pieces(k, group(k) * NX + (x + 2) % NX)
        remote(low, low, fr_snd.at[k], fr_rcv.at[k], at_x(1)).wait_recv()
        remote(high, high, fl_snd.at[k], fl_rcv.at[k], at_x(-1)).wait_recv()

    def side_block(g):
        return rows.at[pl.ds(0, side), pl.ds(pl.multiple_of(g * span, span), span), :]

    def side_on(hop):
        if hop < DOWN_STEPS:
            block = side_block((y + hop) % NY)
            send(block, block, sd_snd.at[hop], sd_rcv.at[hop], at_y(-1))
        if hop < UP_STEPS:
            block = side_block((y - hop + NY) % NY)
            send(block, block, su_snd.at[hop], su_rcv.at[hop], at_y(1))

    def side_in(hop):
        if hop <= UP_STEPS:
            block = side_block((y - hop + NY) % NY)
            remote(block, block, su_snd.at[hop - 1], su_rcv.at[hop - 1], at_y(1)).wait_recv()
        if hop <= DOWN_STEPS:
            block = side_block((y + hop) % NY)
            remote(block, block, sd_snd.at[hop - 1], sd_rcv.at[hop - 1], at_y(-1)).wait_recv()

    def span_of(k):
        return pl.ds(pl.multiple_of(group(k) * span, span), span)

    nt = (((1,), (1,)), ((), ()))

    def multiply(k):
        here = span_of(k)
        acc = jnp.zeros((span, 2 * units), F32)
        for j in range(NZ * planes // 2):
            a, b = 2 * j, 2 * j + 1
            lhs = jnp.concatenate([rows[a, here, :], rows[b, here, :]], axis=1)
            rhs = jnp.concatenate(
                [
                    wcat[a // planes, :, (a % planes) * LANES : (a % planes + 1) * LANES],
                    wcat[b // planes, :, (b % planes) * LANES : (b % planes + 1) * LANES],
                ],
                axis=1,
            )
            acc = acc + lax.dot_general(lhs, rhs, nt, preferred_element_type=F32)
        part[here, :] = acc

    def to_sibling(k):
        here = span_of(k)
        send(part.at[here, :], part_in.at[here, :], p_snd.at[k], p_rcv.at[k], sib)

    partner_tok = (((expert ^ flip) * 2 + (y % 2)) * NX) + x

    def joined(k):
        here = span_of(k)
        remote(part.at[here, :], part_in.at[here, :], p_snd.at[k], p_rcv.at[k], sib).wait_recv()
        both = part[here, :] + part_in[here, :]
        full[here, :] = both
        swap[here, :] = both.astype(BF16)

    def at(off):
        g = (y + off + NY) % NY
        return g, pl.ds(pl.multiple_of(g * span, span), span)

    def swap_copy(off):
        g, here = at(off)
        return remote(swap.at[here, :], swap_in.at[here, :], e_snd.at[g], e_rcv.at[g], (partner_tok, exp))

    def to_partner(k):
        @pl.when(core == 1)
        def _():
            swap_copy(plain_order[k]).start()

    lane = lane[:1]
    zero = jnp.zeros((1, LANES), F32)
    freq_v, label_v = zero, jnp.full((1, LANES), -1, jnp.int32)
    own_label = jnp.int32(0)
    for e in range(EXPERTS):
        freq_v = jnp.where(lane == e, freq[e].astype(F32), freq_v)
        label_v = jnp.where(lane == e, labels[e], label_v)
        own_label = jnp.where(expert == e, labels[e], own_label)
    member = jnp.where(label_v == own_label, 1.0, 0.0).astype(F32)
    member_freq = member * freq_v
    coef = member_freq / jnp.sum(member_freq, axis=1, keepdims=True)
    own_lane = jnp.where(lane == expert, 1.0, 0.0).astype(F32)
    own = jnp.sum(coef * own_lane, axis=1, keepdims=True)
    other = jnp.sum(coef * (1.0 - own_lane), axis=1, keepdims=True)
    taken = jnp.where(core == 1, own * member, own_lane)

    def activate(off):
        g, here = at(off)

        @pl.when(core == 1)
        def _():
            swap_copy(off).wait_recv()
            v = own * full[here, :] + other * swap_in[here, :].astype(F32)
            full[here, :] = v

        v = full[here, :]
        gate, upper = v[:, :units], v[:, units:]
        hid[z, here, :] = (gate / (1.0 + jnp.exp(-gate)) * upper).astype(BF16)

    def along_z(off):
        g, here = at(off)
        for d in (4, 3, 5, 2, 6, 1, 7):
            remote(hid.at[z, here, :], hid.at[z, here, :], h_snd.at[g], h_rcv.at[g], at_z(d)).start()

    def seven(off):
        return hid.at[pl.ds(0, NZ - 1), at(off)[1], :]

    def x_copy(off, d):
        g, _ = at(off)
        there = (x + d) % NX
        part_rows = pl.ds(pl.multiple_of(there * tok_dev, tok_dev), tok_dev)
        return remote(xsend.at[g, part_rows, :], xrecv.at[g, NX - d], x_snd.at[g], x_rcv.at[g], at_x(d))

    def three(off):
        return xrecv.at[at(off)[0], pl.ds(1, NX - 1)]

    def y_copy(off):
        g, _ = at(off)
        return remote(ysend.at[g], yrecv.at[y], y_snd.at[g], y_rcv.at[y], (g * NX + x, exp))

    def finish(off):
        g, here = at(off)
        pltpu.make_async_copy(seven(off), seven(off), h_rcv.at[g]).wait()
        acc = jnp.zeros((span, 2 * width), F32)
        for j in range(NZ // 2):
            lhs = jnp.concatenate([hid[2 * j, here, :], hid[2 * j + 1, here, :]], axis=1)
            acc = acc + jnp.dot(
                lhs, wd[2 * j * units : 2 * (j + 1) * units, :], preferred_element_type=F32
            )
        weight = jnp.sum(rows[NZ * planes, here, :].astype(F32) * taken, axis=1, keepdims=True)
        acc = acc * weight
        xsend[g] = acc.astype(BF16)
        acc_mine[...] = acc
        xown[g] = acc_mine[pl.ds(pl.multiple_of(x * tok_dev, tok_dev), tok_dev), :]
        for d in (2, 1, 3):
            x_copy(off, d).start()

    def reduce(off):
        g, _ = at(off)
        pltpu.make_async_copy(three(off), three(off), x_rcv.at[g]).wait()
        acc = xown[g]
        for d in range(1, NX):
            acc = acc + xrecv[g, d].astype(F32)
        xown[g] = acc
        ysend[g] = acc.astype(BF16)

        @pl.when(g != y)
        def _():
            y_copy(off).start()

    def both_cores(action, plain, paired):
        for i in range(max(len(plain), len(paired))):
            if i < len(plain) and i < len(paired):
                action(jnp.where(core == 1, paired[i], plain[i]))
            elif i < len(plain):
                pl.when(core == 0)(functools.partial(action, plain[i]))
            else:
                pl.when(core == 1)(functools.partial(action, paired[i]))

    def due(step):
        plain = [plain_order[k] for k in range(NY) if k + 2 == step]
        return plain, [pair_order[k] for k in range(NY) if pair_step[k] == step]

    spread(rows.at[pl.ds(NZ * planes, 1), mine, :], tok >= 0)
    spread(own_planes, z >= SIDE)
    for k in (1, 7, 2, 6, 3, 5, 4):
        zz = (z - k + NZ) % NZ
        got = rows.at[pl.ds(zz * planes, planes), mine, :]
        remote(got, got, z_snd.at[k], z_rcv.at[k], at_z(k)).wait_recv()
        spread(got, zz >= SIDE)
    block = rows_of(tok)
    sent.append(remote(block, block, xr_snd.at[0], xr_rcv.at[0], at_x(1)))
    sent.append(remote(block, block, xl_snd.at[0], xl_rcv.at[0], at_x(-1)))
    block = rows_of(tok, side, main)
    sent.append(remote(block, block, up_snd.at[0], up_rcv.at[0], at_y(1)))
    sent.append(remote(block, block, dn_snd.at[0], dn_rcv.at[0], at_y(-1)))
    for copy in loads:
        copy.wait()
    ahead = 1
    hops = NY // 2
    last = max(pair_step) + LAG + SUM_LAG
    for k in range(last + 1):
        late = k > NY
        if k + 1 <= hops:
            from_y(k + 1)
            along_y(k + 1)
        while ahead < NY and ahead <= k + 2 and HOPS[far][ahead] <= k + 1:
            along_x(ahead)
            ahead += 1
        if 0 <= k - 2 < NY:
            joined(k - 2)
        if k == 2 + LAG:
            theirs = wd.at[:, pl.ds(pl.multiple_of((1 - core) * width, LANES), width)]
            remote(theirs, theirs, w_snd.at[2 * NZ], w_rcv.at[2 * NZ], sib).wait_recv()
        if not late:
            both_cores(reduce, *due(k - LAG - SUM_LAG))
            both_cores(finish, *due(k - LAG))
        if 0 <= k - 2 < NY:
            to_partner(k - 2)
        both_cores(activate, *due(k))
        if k < NY:
            from_x(k)
        both_cores(along_z, *due(k))
        if k == 1:
            for zz in range(NZ):
                for which in range(2):
                    i = 2 * zz + which
                    dst = wcat.at[zz, pl.ds(pl.multiple_of(which * units + (1 - core) * half, half), half), :]
                    remote(dst, dst, w_snd.at[i], w_rcv.at[i], sib).wait_recv()
        if 0 <= k - 1 < NY:
            from_far(k - 1)
            if k == 1:
                side_on(0)
            elif k - 1 <= hops:
                side_in(k - 1)
                side_on(k - 1)
            multiply(k - 1)
            to_sibling(k - 1)
        if late:
            both_cores(finish, *due(k - LAG))
            both_cores(reduce, *due(k - LAG - SUM_LAG))

    acc = xown[y]
    for k in range(1, NY):
        g = (y + k) % NY
        remote(ysend.at[g], yrecv.at[g], y_snd.at[g], y_rcv.at[g], at_y(k)).wait_recv()
        acc = acc + yrecv[g].astype(F32)
    kept = jnp.where(core == 0, acc[:, :width], acc[:, width:]).astype(BF16)
    fsend[...] = jnp.where(core == 0, acc[:, width:], acc[:, :width]).astype(BF16)
    send(fsend, frecv, f_snd, f_rcv, sib)
    remote(fsend, frecv, f_snd, f_rcv, sib).wait_recv()
    back = frecv[...]
    first_out[...] = jnp.where(core == 0, kept, back)
    second_out[...] = jnp.where(core == 0, back, kept)

    for copy in zs + gifts + sent:
        copy.wait_send()
    for off in range(NY):
        g, _ = at(off)
        pltpu.make_async_copy(seven(off), seven(off), h_snd.at[g]).wait()
        pltpu.make_async_copy(three(off), three(off), x_snd.at[g]).wait()
        if off > 0:
            y_copy(off).wait_send()

    @pl.when(core == 1)
    def _():
        for off in range(NY):
            swap_copy(off).wait_send()


def local(tokens, route_ids, gate_codes, merge_labels, freq_counts, w_gate, w_up, w_down):
    tok_dev, width = tokens.shape
    half = w_gate.shape[0]
    count, depth = NX * NY * tok_dev, w_down.shape[0]
    units = 2 * half
    planes = width // LANES
    span = NX * tok_dev
    dma = pltpu.SemaphoreType.DMA
    ids_shape = route_ids.shape[::-1]
    scratch = [
        pltpu.SMEM((EXPERTS,), jnp.int32),
        pltpu.SMEM((EXPERTS,), jnp.int32),
        pltpu.VMEM(ids_shape, jnp.int32),
        pltpu.VMEM(ids_shape, jnp.int32),
        pltpu.VMEM((NZ * planes + 1, count, LANES), BF16),
        pltpu.VMEM((NZ, 2 * units, width), BF16),
        pltpu.VMEM((depth, 2 * width), BF16),
        pltpu.VMEM((count, 2 * units), F32),
        pltpu.VMEM((count, 2 * units), F32),
        pltpu.VMEM((count, 2 * units), F32),
        pltpu.VMEM((count, 2 * units), BF16),
        pltpu.VMEM((count, 2 * units), BF16),
        pltpu.VMEM((NZ, count, units), BF16),
        pltpu.VMEM((NY, span, 2 * width), BF16),
        pltpu.VMEM((NY, NX, tok_dev, 2 * width), BF16),
        pltpu.VMEM((NY, tok_dev, 2 * width), F32),
        pltpu.VMEM((span, 2 * width), F32),
        pltpu.VMEM((NY, tok_dev, 2 * width), BF16),
        pltpu.VMEM((NY, tok_dev, 2 * width), BF16),
        pltpu.VMEM((tok_dev, width), BF16),
        pltpu.VMEM((tok_dev, width), BF16),
        dma((4,)),
        dma((planes,)),
        dma((2 * NZ + 1,)),
        dma((2 * NZ + 1,)),
        dma((2 * NZ + 1,)),
        dma((NZ,)),
        dma((NZ,)),
        *[dma((NY // 2,))] * 4,
        *[dma((NY,))] * 16,
        dma((NY,)),
        dma((NY,)),
        dma(()),
        dma(()),
        *[dma((NY // 2,))] * 4,
    ]
    hbm = pl.BlockSpec(memory_space=pltpu.HBM)
    vmem = pl.BlockSpec(memory_space=pltpu.VMEM)
    out = jax.ShapeDtypeStruct((tok_dev, width), BF16)

    def variant(flip):
        def run(*args):
            return pl.pallas_call(
                functools.partial(kernel, flip),
                out_shape=(out, out),
                in_specs=[hbm] * 8,
                out_specs=(vmem, vmem),
                scratch_shapes=scratch,
                compiler_params=pltpu.CompilerParams(
                    collective_id=flip, has_side_effects=True, vmem_limit_bytes=67043328
                ),
                name=f"layer_flip{flip}",
            )(*args)

        return run

    spot = jnp.maximum(jnp.arange(EXPERTS, dtype=jnp.int32) - 1, 0)
    pairing = jnp.sum(jnp.where(merge_labels == merge_labels[0], spot, 0))
    return lax.switch(
        pairing,
        [variant(1), variant(2), variant(3)],
        merge_labels, freq_counts, route_ids.T, gate_codes.T, tokens, w_gate, w_up, w_down,
    )


def solution(mesh):
    return jax.shard_map(
        local,
        mesh=mesh,
        in_specs=(
            P("tok", "exp"),
            P("tok", None),
            P("tok", None),
            P(),
            P(),
            P(("tok", "exp"), None),
            P(("tok", "exp"), None),
            P("tok", "exp"),
        ),
        out_specs=(P("tok", "exp"), P("tok", "exp")),
        check_vma=False,
    )
```
